256 devices in a mesh: row: 32 (over z, x), col: 8 (over y, core).
Axes of the slice: x: 4, y: 4, z: 8, core: 2. Of those that a mesh axis runs over, the one named last changes fastest.
Arguments:
- features: bfloat16 [65536, 256], P(('row', 'col')), may hold values from -6 to 6
- grad_out: bfloat16 [65536, 256], P(('row', 'col')), may hold values from -6 to 6
- degrees: int32 [65536], P(('row', 'col')), may hold values from 1 to 65624, as said below
- w_self: bfloat16 [256, 256], replicated, may hold values from -0.375 to 0.375
- w_neigh: bfloat16 [256, 256], replicated, may hold values from -0.375 to 0.375
- bias: float32 [256], replicated, may hold values from -4 to 4
- tile_slots: int32 [32, 8, 176], P('row', 'col'), may hold values from 0 to 1023, as said below
- tile_count: int32 [32, 8], P('row', 'col'), may hold values from 44 to 176, as said below
- tile_masks: int32 [32, 8, 176, 16, 128], P('row', 'col'), may hold values from 0 to 255
Outputs:
- layer_out: bfloat16 [65536, 256], P(('row', 'col'))
- grad_in: bfloat16 [65536, 256], P(('row', 'col'))
- grad_w_self: float32 [256, 256], replicated
- grad_w_neigh: float32 [256, 256], replicated
The draws below stay inside these ranges and needn't reach their ends.
Inputs may be any that keep to these rules, and one draw needn't show every extreme that they name: `tile_slots`: on each device the 176 slot numbers are distinct and rise; slot s names block row s % 16 of the device's row group and block column s // 16 of its panel. Only a device's first tile_count tiles are live; the others are ignored. Some device holds 176 live tiles. `degrees`: each node's degree is at least the number of ones in its row of A, and at least 1; some node has the largest degree.
All inputs are finite; a program needn't handle non-finite values.
Results may differ from the reference program's by a relative error of at most 0.014.
Values may be sent and summed in bfloat16 or wider, within the bound.
A program may use at most 64 MiB of HBM per device.

```python
import jax
import jax.numpy as jnp
from jax import lax

F = 256
B = 128
R = 256
TPR = 11
WORDS = 16
RB = 16
CB = 64
TPD = 176
NODES = 65536
N_ROW = 32
N_COL = 8


def draw_tile_slots(key, part):
    device_keys = jax.random.split(key, N_ROW * N_COL)
    chosen = jax.vmap(lambda device_key: jax.random.permutation(device_key, RB * CB)[:TPD])(device_keys)
    return jnp.sort(chosen, axis=-1).astype(jnp.int32).reshape(N_ROW, N_COL, TPD)


def draw_tile_count(key, part):
    divisors = jax.random.randint(key, (N_ROW * N_COL,), 1, 5, dtype=jnp.int32)
    counts = TPD // divisors
    busiest = jax.random.randint(jax.random.fold_in(key, 7), (), 0, N_ROW * N_COL, dtype=jnp.int32)
    counts = counts.at[busiest].set(TPD)
    return counts.astype(jnp.int32).reshape(N_ROW, N_COL)


def mask_parts(key):
    device_keys = jax.random.split(jax.random.fold_in(key, 11), N_ROW * N_COL)
    powers = jnp.left_shift(jnp.ones((8,), jnp.int32), jnp.arange(8, dtype=jnp.int32))

    def one_device(device_key):
        draws = jax.random.randint(device_key, (TPD, WORDS, 8, B), 0, 64, dtype=jnp.int32)
        bits = (draws == 0).astype(jnp.int32)
        words = jnp.sum(bits * powers[None, None, :, None], axis=2).astype(jnp.int32)
        row_ones = jnp.sum(bits, axis=(1, 2)).astype(jnp.int32)
        return (words, row_ones)
    words, row_ones = lax.map(one_device, device_keys)
    return (words, row_ones)


def draw_tile_masks(key, part):
    words, _ = mask_parts(key)
    return words.reshape(N_ROW, N_COL, TPD, WORDS, B).astype(jnp.int32)


def draw_degrees(key, part):
    device_count = N_ROW * N_COL
    slots = draw_tile_slots(key, part).reshape(device_count, TPD)
    counts = draw_tile_count(key, part).reshape(device_count)
    _, row_ones = mask_parts(key)
    positions = jnp.arange(TPD, dtype=jnp.int32)
    live = (positions[None, :] < counts[:, None]).astype(jnp.int32)
    row_ones = row_ones * live[:, :, None]
    device_rows = (jnp.arange(device_count, dtype=jnp.int32) // N_COL)[:, None]
    block_index = (device_rows * RB + slots % RB).astype(jnp.int32)
    totals = jnp.zeros((N_ROW * RB, B), jnp.int32).at[block_index.reshape(-1)].add(row_ones.reshape(device_count * TPD, B))
    outside_most = max(1, N_COL * TPR * B // 128)
    outside = jax.random.randint(jax.random.fold_in(key, 13), (NODES,), 1, outside_most + 1, dtype=jnp.int32)
    result = (totals.reshape(NODES) + outside).astype(jnp.int32)
    largest = N_COL * min(TPD, CB) * B + outside_most
    chosen_node = jax.random.randint(jax.random.fold_in(key, 17), (), 0, NODES, dtype=jnp.int32)
    result = result.at[chosen_node].set(jnp.int32(largest))
    return result.astype(jnp.int32)


def block_scale(own_key, shape, cuts, least, high):
    factor_of, own = 1.0, jax.random.fold_in(own_key, 6)
    for position, blocks in cuts:
        steps = jnp.exp(jax.random.uniform(jax.random.fold_in(own, position), (blocks,), jnp.float32, least / len(cuts), high / len(cuts)))
        factor_of = factor_of * jnp.repeat(steps, shape[position] // blocks).reshape([-1 if axis == position else 1 for axis in range(len(shape))])
    return factor_of


def noise(stream_key, shape, width, bound, shards=(), kind=jnp.bfloat16):
    values = jax.random.normal(stream_key, shape, jnp.float32) * width
    if len(shards) > 0:
        values = block_scale(stream_key, shape, shards, -0.22, 0.18) * values
    return jnp.clip(values, min=-bound, max=bound).astype(kind)


def setup_inputs(seed: int = 0) -> dict:
    key_list = jax.random.split(jax.random.key(seed), 10)
    features = noise(key_list[0], (NODES, F), 1.0, 6.0, ((0, 256),))
    grad_out = noise(key_list[1], (NODES, F), 1.0, 6.0, ((0, 256),))
    degrees = draw_degrees(jax.random.fold_in(key_list[9], 71), 0)
    w_self = noise(key_list[3], (F, F), F ** -0.5, 0.375)
    w_neigh = noise(key_list[4], (F, F), F ** -0.5, 0.375)
    bias = noise(key_list[5], (F,), 1.0, 4.0, (), jnp.float32)
    tile_slots = draw_tile_slots(jax.random.fold_in(key_list[9], 71), 0)
    tile_count = draw_tile_count(jax.random.fold_in(key_list[9], 71), 0)
    tile_masks = draw_tile_masks(jax.random.fold_in(key_list[9], 71), 0)
    return {"features": features, "grad_out": grad_out, "degrees": degrees, "w_self": w_self, "w_neigh": w_neigh, "bias": bias, "tile_slots": tile_slots, "tile_count": tile_count, "tile_masks": tile_masks}


def unpack_tiles(mask_words):
    shifts = jnp.arange(8, dtype=jnp.int32)
    bit_values = jnp.bitwise_and(jnp.right_shift(mask_words[:, :, None, :], shifts[None, None, :, None]), 1)
    return bit_values.reshape(mask_words.shape[0], mask_words.shape[1] * 8, mask_words.shape[2])


def reference(features, grad_out, degrees, w_self, w_neigh, bias, tile_slots, tile_count, tile_masks):
    device_count = N_ROW * N_COL
    slot_table = tile_slots.reshape(device_count, TPD)
    count_table = tile_count.reshape(device_count)
    mask_table = tile_masks.reshape(device_count, TPD, WORDS, B)
    positions = jnp.arange(TPD, dtype=jnp.int32)
    panels = features.reshape(N_ROW, N_COL, R, F)
    device_ids = jnp.arange(device_count, dtype=jnp.int32)

    def device_tiles(device):
        slot_ids = slot_table[device]
        is_live = (positions < count_table[device]).astype(jnp.float32)
        tile_bits = unpack_tiles(mask_table[device]).astype(jnp.float32) * is_live[:, None, None]
        return tile_bits, slot_ids % RB, slot_ids // RB

    def forward_step(summed, device):
        row_index = device // N_COL
        col_index = device % N_COL
        tile_bits, row_block, column_block = device_tiles(device)
        panel = lax.dynamic_index_in_dim(panels, col_index, axis=1, keepdims=False).reshape(CB, B, F)
        sources = panel[column_block].astype(jnp.float32)
        products = jnp.einsum("tji,tjf->tif", tile_bits, sources, precision=lax.Precision.HIGHEST)
        partial_value = jnp.zeros((RB, B, F), jnp.float32).at[row_block].add(products)
        partial_value = lax.optimization_barrier(partial_value.astype(jnp.bfloat16)).astype(jnp.float32)
        return summed.at[row_index].add(partial_value.reshape(RB * B, F)), None

    summed, _ = lax.scan(forward_step, jnp.zeros((N_ROW, RB * B, F), jnp.float32), device_ids)
    summed = summed.reshape(NODES, F)
    scale_degree = degrees.astype(jnp.float32)[:, None]
    mean_rows = (summed / scale_degree).astype(jnp.bfloat16)
    preact = jnp.dot(features, w_self, preferred_element_type=jnp.float32)
    preact = preact + jnp.dot(mean_rows, w_neigh, preferred_element_type=jnp.float32) + bias
    sigmoid_values = jax.nn.sigmoid(preact)
    layer_out = (preact * sigmoid_values).astype(jnp.bfloat16)
    grad_preact = (grad_out.astype(jnp.float32) * sigmoid_values * (1.0 + preact * (1.0 - sigmoid_values))).astype(jnp.bfloat16)
    grad_scale = NODES ** -0.5
    grad_w_self = jnp.dot(features.T, grad_preact, preferred_element_type=jnp.float32) * grad_scale
    grad_w_neigh = jnp.dot(mean_rows.T, grad_preact, preferred_element_type=jnp.float32) * grad_scale
    upward = (jnp.dot(grad_preact, w_neigh.T, preferred_element_type=jnp.float32) / scale_degree).astype(jnp.bfloat16)
    upward_groups = upward.reshape(N_ROW, RB, B, F)

    def backward_step(spread, device):
        row_index = device // N_COL
        col_index = device % N_COL
        tile_bits, row_block, column_block = device_tiles(device)
        group_rows = lax.dynamic_index_in_dim(upward_groups, row_index, axis=0, keepdims=False)
        sources = group_rows[row_block].astype(jnp.float32)
        products = jnp.einsum("tji,tif->tjf", tile_bits, sources, precision=lax.Precision.HIGHEST)
        partial_value = jnp.zeros((CB, B, F), jnp.float32).at[column_block].add(products)
        partial_value = lax.optimization_barrier(partial_value.astype(jnp.bfloat16)).astype(jnp.float32)
        return spread.at[col_index].add(partial_value.reshape(N_ROW, R, F)), None

    spread, _ = lax.scan(backward_step, jnp.zeros((N_COL, N_ROW, R, F), jnp.float32), device_ids)
    neighbor_grad = jnp.transpose(spread, (1, 0, 2, 3)).reshape(NODES, F)
    grad_in = (jnp.dot(grad_preact, w_self.T, preferred_element_type=jnp.float32) + neighbor_grad).astype(jnp.bfloat16)
    return layer_out, grad_in, grad_w_self, grad_w_neigh
```

```python
import functools
import heapq
import math

import jax
import jax.numpy as jnp
from jax import lax
from jax.experimental import pallas as pl
from jax.experimental.pallas import tpu as pltpu
from jax.sharding import PartitionSpec as P

MESH = pl.DeviceIdType.MESH
SMEM = pl.BlockSpec(memory_space=pltpu.SMEM)
VMEM = pl.BlockSpec(memory_space=pltpu.VMEM)
ANY = pl.BlockSpec(memory_space=pl.ANY)
TILE = 128
UNROLL = 16
VMEM_BYTES = 60 << 20


def torus_plan(nx, nz, split, latency=1.0, rate=0.01):
    size = {"x": nx, "z": nz}
    transfers, entries, order = [], {}, []
    free, heap = {}, []

    def wrap(d, n):
        d %= n
        return d - n if d > n // 2 else d

    def send(now, node, axis, sign, first, count):
        offset = {"x": node[1], "z": node[2]}
        offset[axis] = wrap(offset[axis] - sign, size[axis])
        index = len(transfers)
        transfers.append((axis, sign, first, count, (node[0], offset["x"], offset["z"])))
        start = max(now, free.get((axis, sign), 0.0))
        free[axis, sign] = start + count * rate
        heapq.heappush(heap, (free[axis, sign] + latency, index))
        entries[node][1].append(index)

    def forward(now, node):
        part = node[0]
        begin, full = (0, split[0]) if part == 0 else (split[0], split[1])
        offset = {"x": node[1], "z": node[2]}
        p, q = ("x", "z") if part == 0 else ("z", "x")
        dp, dq = offset[p], offset[q]
        half_p, half_q = size[p] // 2, size[q] // 2
        lower = (full // 2 + 15) // 16 * 16
        for sign in (1, -1):
            if dq == 0 and (dp == 0 or -dp * sign > 0) and dp != half_p:
                if abs(dp) + 1 < half_p:
                    send(now, node, p, sign, begin, full)
                elif sign == 1:
                    send(now, node, p, sign, begin, lower)
                else:
                    send(now, node, p, sign, begin + lower, full - lower)
        for sign in (1, -1):
            if (dq == 0 or -dq * sign > 0) and dq != half_q:
                if abs(dq) + 1 < half_q or (0 <= dp < half_p) == (sign == 1):
                    send(now, node, q, sign, begin, full)

    got = {}
    for part in (0, 1):
        entries[part, 0, 0] = ([], [])
        order.append((part, 0, 0))
        forward(0.0, (part, 0, 0))
    while heap:
        now, index = heapq.heappop(heap)
        count, node = transfers[index][3:]
        entries.setdefault(node, ([], []))[0].append(index)
        got[node] = got.get(node, 0) + count
        if got[node] == split[node[0]]:
            order.append(node)
            forward(now, node)
    return transfers, [(node, *entries[node]) for node in order]


class Torus:
    def __init__(self, nx, nz):
        self.nx, self.nz = nx, nz
        row = lax.axis_index("row")
        self.x, self.z = lax.rem(row, nx), lax.div(row, nx)

    def row(self, dx, dz):
        x = lax.rem(self.x + (dx + self.nx), self.nx)
        z = lax.rem(self.z + (dz + self.nz), self.nz)
        return z * self.nx + x

    def neighbour(self, axis, sign):
        return {"row": self.row(sign, 0) if axis == "x" else self.row(0, sign)}


def greet(barrier, peers):
    for peer in peers:
        pl.semaphore_signal(barrier, inc=1, device_id=peer, device_id_type=MESH)


def row_order(size):
    place = lax.broadcasted_iota(jnp.int32, (size, size), 0)
    node = lax.broadcasted_iota(jnp.int32, (size, size), 1)
    within = place & (TILE - 1)
    source = (place - within) + ((within & 15) << 3) + (within >> 4)
    return jnp.where(source == node, 1.0, 0.0).astype(jnp.bfloat16)


def gather_kernel(transfers, order, nx, nz, features, panel, own, local_sem, send_sem, recv_sem):
    torus = Torus(nx, nz)
    me = torus.row(0, 0)
    barrier = pltpu.get_barrier_semaphore()
    around = [torus.neighbour(axis, sign) for axis in "xz" for sign in (1, -1)]
    greet(barrier, around)
    own[...] = jnp.dot(
        row_order(own.shape[0]), features[...], preferred_element_type=jnp.float32
    ).astype(own.dtype)
    pl.semaphore_wait(barrier, len(around))

    def copy(index, node, source):
        axis, sign, first, count, _ = transfers[index]
        origin = torus.row(node[1], node[2])
        rows = pl.ds(first, count)
        return pltpu.make_async_remote_copy(
            src_ref=own.at[rows] if source else panel.at[origin, rows],
            dst_ref=panel.at[origin, rows],
            send_sem=send_sem.at[index],
            recv_sem=recv_sem.at[index],
            device_id=torus.neighbour(axis, sign),
            device_id_type=MESH,
        )

    started = []
    for node, brought, carried in order:
        for index in brought:
            copy(index, node, False).wait_recv()
        for index in carried:
            started.append(copy(index, node, not brought))
            started[-1].start()
    keep = pltpu.make_async_copy(own, panel.at[me], local_sem)
    keep.start()
    for each in started:
        each.wait_send()
    keep.wait()


def unpack(words):
    return jnp.concatenate(
        [((words >> bit) & 1).astype(jnp.float32).astype(jnp.bfloat16) for bit in range(8)], axis=0
    )


def each_tile(slots, live, masks, block_rows, step):
    last = masks.shape[0] - 1

    def group(index, _):
        for u in range(UNROLL):
            tile = index * UNROLL + u
            held = jnp.minimum(tile, last)
            slot = slots[held]
            words = jnp.where(tile < live, masks[held], 0)
            step(lax.rem(slot, block_rows), lax.div(slot, block_rows), unpack(words))
        return 0

    lax.fori_loop(0, lax.div(live + (UNROLL - 1), UNROLL), group, 0)


def set_zero(total):
    def one(i, _):
        total[i] = jnp.zeros(total.shape[1:], total.dtype)
        return 0

    lax.fori_loop(0, total.shape[0], one, 0)


def round_to(out, total):
    def one(i, _):
        out[i] = total[i].astype(out.dtype)
        return 0

    lax.fori_loop(0, total.shape[0], one, 0)


def aggregate_kernel(slots, count, masks, panel, out, total):
    set_zero(total)

    def step(row_block, column_block, bits):
        total[row_block] += lax.dot_general(
            bits, panel[column_block], (((0,), (0,)), ((), ())), preferred_element_type=jnp.float32
        )

    each_tile(slots, count[0], masks, out.shape[0], step)
    round_to(out, total)


def spread_kernel(slots, count, masks, upward, out, total):
    set_zero(total)

    def step(row_block, column_block, bits):
        total[column_block] += jnp.dot(bits, upward[row_block], preferred_element_type=jnp.float32)

    each_tile(slots, count[0], masks, upward.shape[0], step)
    round_to(out, total)


def middle_kernel(
    n_col, partial, features, grad_out, degrees, w_self, w_neigh, bias,
    layer_out, grad_preact, upward_rows, grad_sums,
    arrived, upward, weight_parts, weight_arrived,
    local_sem, sum_send, sum_recv, up_send, up_recv, weight_send, weight_recv,
):
    col = lax.axis_index("col")
    peers = [lax.rem(col + k, n_col) for k in range(n_col)]
    barrier = pltpu.get_barrier_semaphore()
    greet(barrier, [{"col": peer} for peer in peers[1:]])
    size, width = features.shape
    scale = jnp.broadcast_to(degrees[...].astype(jnp.float32), (width, size)).T
    own_part = jnp.dot(features[...], w_self[...], preferred_element_type=jnp.float32)
    pl.semaphore_wait(barrier, n_col - 1)

    def remote(source, target, sends, recvs, k):
        return pltpu.make_async_remote_copy(
            src_ref=source,
            dst_ref=target,
            send_sem=sends.at[k - 1],
            recv_sem=recvs.at[k - 1],
            device_id={"col": peers[k]},
            device_id_type=MESH,
        )

    started = []
    for k in range(1, n_col):
        started.append(remote(partial.at[peers[k]], arrived.at[k - 1], sum_send, sum_recv, k))
        started[-1].start()
    summed = partial[col].astype(jnp.float32)
    for k in range(1, n_col):
        started[k - 1].wait_recv()
        summed = summed + arrived[k - 1].astype(jnp.float32)
    mean_rows = (summed / scale).astype(jnp.bfloat16)
    preact = own_part + jnp.dot(mean_rows, w_neigh[...], preferred_element_type=jnp.float32)
    preact = preact + bias[...]
    sigmoid_values = jax.nn.sigmoid(preact)
    layer_out[...] = (preact * sigmoid_values).astype(layer_out.dtype)
    gradient = (
        grad_out[...].astype(jnp.float32) * sigmoid_values * (1.0 + preact * (1.0 - sigmoid_values))
    ).astype(jnp.bfloat16)
    grad_preact[...] = gradient
    sent_up = lax.dot_general(
        gradient, w_neigh[...], (((1,), (1,)), ((), ())), preferred_element_type=jnp.float32
    )
    upward[...] = (sent_up / scale).astype(upward.dtype)
    first_up = len(started)
    for k in range(1, n_col):
        started.append(remote(upward, upward_rows.at[col], up_send, up_recv, k))
        started[-1].start()
    keep = pltpu.make_async_copy(upward, upward_rows.at[col], local_sem)
    keep.start()

    contract_rows = (((0,), (0,)), ((), ()))
    rows = width // n_col
    for half, source in enumerate((features[...], mean_rows)):
        product = lax.dot_general(source, gradient, contract_rows, preferred_element_type=jnp.float32)
        product = product.astype(weight_parts.dtype)
        for c in range(n_col):
            weight_parts[c, half * rows : (half + 1) * rows] = product[c * rows : (c + 1) * rows]
    first_weight = len(started)
    for k in range(1, n_col):
        started.append(
            remote(weight_parts.at[peers[k]], weight_arrived.at[k - 1], weight_send, weight_recv, k)
        )
        started[-1].start()
    total = weight_parts[col].astype(jnp.float32)
    for k in range(1, n_col):
        started[first_weight + k - 1].wait_recv()
        total = total + weight_arrived[k - 1].astype(jnp.float32)
    grad_sums[...] = total
    for k in range(1, n_col):
        started[first_up + k - 1].wait_recv()
    for each in started:
        each.wait_send()
    keep.wait()


def scatter_kernel(
    transfers, order, nx, nz, n_col, grad_scale, partial, grad_preact, w_self, grad_sums,
    grad_in, grad_self, grad_neigh,
    total, arrived, z_arrived, x_sums, z_sums, all_sums,
    load_sem, send_sem, recv_sem, z_send, z_recv, x_send, x_recv, zz_send, zz_recv, col_send, col_recv,
):
    torus = Torus(nx, nz)
    col = lax.axis_index("col")
    load = pltpu.make_async_copy(partial, total, load_sem)
    load.start()
    barrier = pltpu.get_barrier_semaphore()
    along_z = [{"row": torus.row(0, k)} for k in range(1, nz)]
    along_x = [{"row": torus.row(k, 0)} for k in range(1, nx)]
    along_col = [{"col": lax.rem(col + k, n_col)} for k in range(1, n_col)]
    greet(barrier, along_z + along_x + along_col)
    moved = jnp.dot(
        row_order(grad_preact.shape[0]), grad_preact[...], preferred_element_type=jnp.float32
    ).astype(jnp.bfloat16)
    self_grad = lax.dot_general(
        moved, w_self[...], (((1,), (1,)), ((), ())), preferred_element_type=jnp.float32
    )
    pl.semaphore_wait(barrier, len(along_z) + len(along_x) + len(along_col))

    started = []

    def start(source, target, sends, recvs, k, peer):
        started.append(
            pltpu.make_async_remote_copy(
                src_ref=source,
                dst_ref=target,
                send_sem=sends.at[k],
                recv_sem=recvs.at[k],
                device_id=peer,
                device_id_type=MESH,
            )
        )
        started[-1].start()
        return started[-1]

    def reduce_along_z():
        return [
            start(grad_sums.at[lax.rem(torus.z + k, nz)], z_arrived.at[k - 1], z_send, z_recv, k - 1, peer)
            for k, peer in enumerate(along_z, 1)
        ]

    def reduce_along_x(before):
        for each in before:
            each.wait_recv()
        part = grad_sums[torus.z]
        for k in range(nz - 1):
            part = part + z_arrived[k]
        x_sums[torus.x] = part
        return [
            start(x_sums.at[torus.x], x_sums.at[torus.x], x_send, x_recv, k, peer)
            for k, peer in enumerate(along_x)
        ]

    def gather_along_z(before):
        for each in before:
            each.wait_recv()
        part = x_sums[0]
        for k in range(1, nx):
            part = part + x_sums[k]
        z_sums[torus.z] = part * grad_scale
        return [
            start(z_sums.at[torus.z], z_sums.at[torus.z], zz_send, zz_recv, k, peer)
            for k, peer in enumerate(along_z)
        ]

    def gather_along_col(before):
        for each in before:
            each.wait_recv()
        all_sums[col] = z_sums[...].reshape(all_sums.shape[1:])
        return [
            start(all_sums.at[col], all_sums.at[col], col_send, col_recv, k, peer)
            for k, peer in enumerate(along_col)
        ]

    def copy(index, node):
        axis, sign, first, count, _ = transfers[index]
        return start(
            total.at[torus.row(node[1], node[2]), pl.ds(first, count)],
            arrived.at[index, pl.ds(0, count)],
            send_sem,
            recv_sem,
            index,
            torus.neighbour(axis, -sign),
        )

    sent = {}
    pending = reduce_along_z()
    stages = {24: reduce_along_x, 36: gather_along_z, 48: gather_along_col}
    load.wait()
    for position, (node, brought, carried) in enumerate(reversed(order)):
        if position in stages:
            pending = stages[position](pending)
        owner = torus.row(node[1], node[2])
        for index in reversed(carried):
            first, count = transfers[index][2:4]
            sent[index].wait_recv()
            if brought:
                rows = pl.ds(first, count)
                total[owner, rows] = (
                    total[owner, rows].astype(jnp.float32)
                    + arrived[index, :count].astype(jnp.float32)
                ).astype(total.dtype)
        for index in reversed(brought):
            sent[index] = copy(index, node)

    me = torus.row(0, 0)
    sums = {}
    for node, brought, carried in order[:2]:
        first = min(transfers[index][2] for index in carried)
        full = max(transfers[index][2] + transfers[index][3] for index in carried) - first
        part = total[me, first : first + full].astype(jnp.float32)
        for index in carried:
            lead, count = transfers[index][2:4]
            came = arrived[index, :count].astype(jnp.float32)
            if count < full:
                filler = jnp.zeros((full - count, came.shape[1]), jnp.float32)
                came = jnp.concatenate([came, filler] if lead == first else [filler, came], axis=0)
            part = part + came
        sums[node[0]] = part
    result = (self_grad + jnp.concatenate([sums[0], sums[1]], axis=0)).astype(jnp.bfloat16)
    grad_in[...] = lax.dot_general(
        row_order(result.shape[0]), result, (((0,), (0,)), ((), ())), preferred_element_type=jnp.float32
    ).astype(grad_in.dtype)
    for each in pending:
        each.wait_recv()
    rows = all_sums.shape[1] // 2
    for c in range(n_col):
        grad_self[c * rows : (c + 1) * rows] = all_sums[c, :rows]
        grad_neigh[c * rows : (c + 1) * rows] = all_sums[c, rows:]
    for each in started:
        each.wait_send()


def shards(features, grad_out, degrees, w_self, w_neigh, bias, tile_slots, tile_count, tile_masks):
    size, width = features.shape
    n_row, n_col = lax.axis_size("row"), lax.axis_size("col")
    nx, nz = 4, n_row // 4
    split = (size // 2, size // 2)
    transfers, order = torus_plan(nx, nz, split)
    copies = len(transfers)
    bf16, f32 = jnp.bfloat16, jnp.float32
    dma = pltpu.SemaphoreType.DMA
    slots, count, masks = tile_slots[0, 0], tile_count[0], tile_masks[0, 0]
    block_rows = size * n_col // TILE
    block_columns = size * n_row // TILE

    def remote(identity):
        return pltpu.CompilerParams(
            collective_id=identity, has_side_effects=True, vmem_limit_bytes=VMEM_BYTES
        )

    panel = pl.pallas_call(
        functools.partial(gather_kernel, transfers, order, nx, nz),
        name="gather_panel",
        out_shape=jax.ShapeDtypeStruct((n_row, size, width), bf16),
        in_specs=[VMEM],
        out_specs=ANY,
        scratch_shapes=[pltpu.VMEM((size, width), bf16), dma, dma((copies,)), dma((copies,))],
        compiler_params=remote(0),
    )(features)

    partial = pl.pallas_call(
        aggregate_kernel,
        name="aggregate",
        out_shape=jax.ShapeDtypeStruct((block_rows, TILE, width), bf16),
        in_specs=[SMEM, SMEM, VMEM, VMEM],
        out_specs=VMEM,
        scratch_shapes=[pltpu.VMEM((block_rows, TILE, width), f32)],
        compiler_params=pltpu.CompilerParams(vmem_limit_bytes=VMEM_BYTES),
    )(slots, count, masks, panel.reshape(block_columns, TILE, width))

    others = n_col - 1
    grad_rows = 2 * width // n_col
    layer_out, grad_preact, upward_rows, grad_sums = pl.pallas_call(
        functools.partial(middle_kernel, n_col),
        name="middle",
        out_shape=(
            jax.ShapeDtypeStruct((size, width), bf16),
            jax.ShapeDtypeStruct((size, width), bf16),
            jax.ShapeDtypeStruct((n_col, size, width), bf16),
            jax.ShapeDtypeStruct((grad_rows, width), f32),
        ),
        in_specs=[VMEM] * 7,
        out_specs=(VMEM, VMEM, ANY, VMEM),
        scratch_shapes=[
            pltpu.VMEM((others, size, width), bf16),
            pltpu.VMEM((size, width), bf16),
            pltpu.VMEM((n_col, grad_rows, width), bf16),
            pltpu.VMEM((others, grad_rows, width), bf16),
            dma,
        ]
        + [dma((others,))] * 6,
        compiler_params=remote(1),
    )(
        partial.reshape(n_col, size, width),
        features,
        grad_out,
        degrees[None, :],
        w_self,
        w_neigh,
        bias[None, :],
    )

    spread = pl.pallas_call(
        spread_kernel,
        name="spread",
        out_shape=jax.ShapeDtypeStruct((block_columns, TILE, width), bf16),
        in_specs=[SMEM, SMEM, VMEM, VMEM],
        out_specs=VMEM,
        scratch_shapes=[pltpu.VMEM((block_columns, TILE, width), f32)],
        compiler_params=pltpu.CompilerParams(vmem_limit_bytes=VMEM_BYTES),
    )(slots, count, masks, upward_rows.reshape(block_rows, TILE, width))

    grad_scale = 1.0 / math.sqrt(size * n_row * n_col)
    z_rows = grad_rows // nz
    grad_in, grad_self, grad_neigh = pl.pallas_call(
        functools.partial(scatter_kernel, transfers, order, nx, nz, n_col, grad_scale),
        name="scatter_panel",
        out_shape=(
            jax.ShapeDtypeStruct((size, width), bf16),
            jax.ShapeDtypeStruct((width, width), f32),
            jax.ShapeDtypeStruct((width, width), f32),
        ),
        in_specs=[ANY, VMEM, VMEM, VMEM],
        out_specs=(VMEM, VMEM, VMEM),
        scratch_shapes=[
            pltpu.VMEM((n_row, size, width), bf16),
            pltpu.VMEM((copies, max(split), width), bf16),
            pltpu.VMEM((nz - 1, z_rows, width), f32),
            pltpu.VMEM((nx, z_rows, width), f32),
            pltpu.VMEM((nz, z_rows, width), f32),
            pltpu.VMEM((n_col, grad_rows, width), f32),
            dma,
            dma((copies,)),
            dma((copies,)),
        ]
        + [dma((nz - 1,))] * 2
        + [dma((nx - 1,))] * 2
        + [dma((nz - 1,))] * 2
        + [dma((others,))] * 2,
        compiler_params=remote(2),
    )(
        spread.reshape(n_row, size, width),
        grad_preact,
        w_self,
        grad_sums.reshape(nz, z_rows, width),
    )
    return (layer_out, grad_in, grad_self, grad_neigh)


def solution(mesh):
    placed = (
        P(("row", "col"), None),
        P(("row", "col"), None),
        P(("row", "col")),
        P(),
        P(),
        P(),
        P("row", "col", None),
        P("row", "col"),
        P("row", "col", None, None, None),
    )
    return jax.shard_map(
        shards,
        mesh=mesh,
        in_specs=placed,
        out_specs=(P(("row", "col"), None), P(("row", "col"), None), P(), P()),
        check_vma=False,
    )
```

```python
import functools
import heapq
import math

import jax
import jax.numpy as jnp
from jax import lax
from jax.experimental import pallas as pl
from jax.experimental.pallas import tpu as pltpu
from jax.sharding import PartitionSpec as P

MESH = pl.DeviceIdType.MESH
SMEM = pl.BlockSpec(memory_space=pltpu.SMEM)
VMEM = pl.BlockSpec(memory_space=pltpu.VMEM)
ANY = pl.BlockSpec(memory_space=pl.ANY)
TILE = 128
UNROLL = 16


def torus_plan(nx, nz, split, latency=1.0, rate=0.01):
    size = {"x": nx, "z": nz}
    transfers, order = [], []
    free, heap = {}, []

    def wrap(d, n):
        d %= n
        return d - n if d > n // 2 else d

    def send(now, node, axis, sign, first, count):
        offset = {"x": node[1], "z": node[2]}
        offset[axis] = wrap(offset[axis] - sign, size[axis])
        index = len(transfers)
        transfers.append((axis, sign, first, count, (node[0], offset["x"], offset["z"])))
        start = max(now, free.get((axis, sign), 0.0))
        free[axis, sign] = start + count * rate
        heapq.heappush(heap, (free[axis, sign] + latency, index))
        entries[node][1].append(index)

    def forward(now, node, phases="pq"):
        part = node[0]
        (p, q), begin, full = split[part]
        offset = {"x": node[1], "z": node[2]}
        dp, dq = offset[p], offset[q]
        half_p, half_q = size[p] // 2, size[q] // 2
        lower = (full // 2 + 15) // 16 * 16
        for sign in (1, -1) if "p" in phases else ():
            if dq == 0 and (dp == 0 or -dp * sign > 0) and dp != half_p:
                if abs(dp) + 1 < half_p:
                    send(now, node, p, sign, begin, full)
                elif sign == 1:
                    send(now, node, p, sign, begin, lower)
                else:
                    send(now, node, p, sign, begin + lower, full - lower)
        for sign in (1, -1) if "q" in phases else ():
            if (dq == 0 or -dq * sign > 0) and dq != half_q:
                if abs(dq) + 1 < half_q or (0 <= dp < half_p) == (sign == 1):
                    send(now, node, q, sign, begin, full)

    got = {}
    entries = {(part, 0, 0): ([], []) for part in range(len(split))}
    roots = []
    for phases in "pq":
        for part in range(len(split)):
            forward(0.0, (part, 0, 0), phases)
            roots.append(((part, 0, 0), [], entries[part, 0, 0][1]))
            entries[part, 0, 0] = ([], [])
    while heap:
        now, index = heapq.heappop(heap)
        count, node = transfers[index][3:]
        entries.setdefault(node, ([], []))[0].append(index)
        got[node] = got.get(node, 0) + count
        if got[node] == split[node[0]][2]:
            order.append(node)
            forward(now, node)
    return transfers, roots + [(node, *entries[node]) for node in order]


class Torus:
    def __init__(self, nx, nz):
        self.nx, self.nz = nx, nz
        row = lax.axis_index("row")
        self.x, self.z = lax.rem(row, nx), lax.div(row, nx)

    def row(self, dx, dz):
        x = lax.rem(self.x + (dx + self.nx), self.nx)
        z = lax.rem(self.z + (dz + self.nz), self.nz)
        return z * self.nx + x

    def neighbour(self, axis, sign):
        return {"row": self.row(sign, 0) if axis == "x" else self.row(0, sign)}


def greet(barrier, peers):
    for peer in peers:
        pl.semaphore_signal(barrier, inc=1, device_id=peer, device_id_type=MESH)


def row_order(size):
    place = lax.broadcasted_iota(jnp.int32, (size, size), 0)
    node = lax.broadcasted_iota(jnp.int32, (size, size), 1)
    within = place & (TILE - 1)
    source = (place - within) + ((within & 15) << 3) + (within >> 4)
    return jnp.where(source == node, 1.0, 0.0).astype(jnp.bfloat16)


def gather_kernel(transfers, order, nx, nz, features, panel, own, local_sem, send_sem, recv_sem):
    torus = Torus(nx, nz)
    me = torus.row(0, 0)
    barrier = pltpu.get_barrier_semaphore()
    around = [torus.neighbour(axis, sign) for axis in "xz" for sign in (1, -1)]
    greet(barrier, around)
    own[...] = jnp.dot(
        row_order(own.shape[0]), features[...], preferred_element_type=jnp.float32
    ).astype(own.dtype)
    pl.semaphore_wait(barrier, len(around))

    def copy(index, node, source):
        axis, sign, first, count, _ = transfers[index]
        origin = torus.row(node[1], node[2])
        rows = pl.ds(first, count)
        return pltpu.make_async_remote_copy(
            src_ref=own.at[rows] if source else panel.at[origin, rows],
            dst_ref=panel.at[origin, rows],
            send_sem=send_sem.at[index],
            recv_sem=recv_sem.at[index],
            device_id=torus.neighbour(axis, sign),
            device_id_type=MESH,
        )

    started = []
    for node, brought, carried in order:
        for index in brought:
            copy(index, node, False).wait_recv()
        for index in carried:
            started.append(copy(index, node, not brought))
            started[-1].start()
    keep = pltpu.make_async_copy(own, panel.at[me], local_sem)
    keep.start()
    for each in started:
        each.wait_send()
    keep.wait()


def unpack(words):
    return jnp.concatenate(
        [((words >> bit) & 1).astype(jnp.float32).astype(jnp.bfloat16) for bit in range(8)], axis=0
    )


def each_tile(slots, live, masks, block_rows, step):
    last = masks.shape[0] - 1

    def group(index, _):
        for u in range(UNROLL):
            tile = index * UNROLL + u
            held = jnp.minimum(tile, last)
            slot = slots[held]
            words = jnp.where(tile < live, masks[held], 0)
            step(lax.rem(slot, block_rows), lax.div(slot, block_rows), unpack(words))
        return 0

    lax.fori_loop(0, lax.div(live + (UNROLL - 1), UNROLL), group, 0)


def set_zero(total):
    def one(i, _):
        total[i] = jnp.zeros(total.shape[1:], total.dtype)
        return 0

    lax.fori_loop(0, total.shape[0], one, 0)


def round_to(out, total):
    def one(i, _):
        out[i] = total[i].astype(out.dtype)
        return 0

    lax.fori_loop(0, total.shape[0], one, 0)


def aggregate_kernel(slots, count, masks, panel, out, total):
    set_zero(total)

    def step(row_block, column_block, bits):
        total[row_block] += lax.dot_general(
            bits, panel[column_block], (((0,), (0,)), ((), ())), preferred_element_type=jnp.float32
        )

    each_tile(slots, count[0], masks, out.shape[0], step)
    round_to(out, total)


def spread_kernel(slots, count, masks, upward, layer_in, out, layer_out, total, layer_sem):
    hand_on = pltpu.make_async_copy(layer_in, layer_out, layer_sem)
    hand_on.start()
    set_zero(total)

    def step(row_block, column_block, bits):
        total[column_block] += jnp.dot(bits, upward[row_block], preferred_element_type=jnp.float32)

    each_tile(slots, count[0], masks, upward.shape[0], step)
    round_to(out, total)
    hand_on.wait()


def middle_kernel(
    partial, features, grad_out, degrees, w_self, w_neigh, bias,
    layer_out, mean_rows, grad_preact, upward_rows,
    own_part, scale, from_sibling, joined, arrived, own_sum, upward,
    keep_sem, sibling_send, sibling_recv, y_send, y_recv, up_send, up_recv, pass_send, pass_recv,
):
    col = lax.axis_index("col")
    y, core = lax.div(col, 2), lax.rem(col, 2)
    ny = partial.shape[0] // 2
    halves, rows = partial.shape[1:3]
    place = [lax.rem(y + k, ny) for k in range(ny)]
    far_first = sorted(range(1, ny), key=lambda k: -min(k, ny - k))
    sibling = {"col": 2 * y + 1 - core}
    along_y = [{"col": 2 * place[k] + core} for k in range(ny)]
    barrier = pltpu.get_barrier_semaphore()
    greet(barrier, [sibling, *along_y[1:]])
    size, width = features.shape
    scale[...] = jnp.broadcast_to(degrees[...].astype(jnp.float32), (width, size)).T
    own_part[...] = bias[...] + jnp.dot(
        features[...], w_self[...], preferred_element_type=jnp.float32
    )
    pl.semaphore_wait(barrier, ny)

    started = []

    def start(source, target, sends, recvs, k, peer):
        copy = pltpu.make_async_remote_copy(
            src_ref=source,
            dst_ref=target,
            send_sem=sends.at[k],
            recv_sem=recvs.at[k],
            device_id=peer,
            device_id_type=MESH,
        )
        copy.start()
        started.append(copy)
        return copy

    pieces = [(half, k) for half in range(halves) for k in (*far_first, 0)]
    shared = {}
    for half, k in pieces:
        shared[half, k] = start(
            partial.at[2 * place[k] + 1 - core, half], from_sibling.at[k, half],
            sibling_send, sibling_recv, half * ny + k, sibling,
        )
    exchanged = {}
    for half, k in pieces:
        shared[half, k].wait_recv()
        both = partial[2 * place[k] + core, half].astype(jnp.float32)
        both = both + from_sibling[k, half].astype(jnp.float32)
        if k == 0:
            own_sum[half] = both
        else:
            joined[k - 1, half] = both.astype(joined.dtype)
            exchanged[half, k] = start(
                joined.at[k - 1, half], arrived.at[k - 1, half],
                y_send, y_recv, half * (ny - 1) + k - 1, along_y[k],
            )
    gathered, passed, kept = {}, [], []
    for half in range(halves):
        summed = own_sum[half]
        for k in far_first:
            exchanged[half, k].wait_recv()
            summed = summed + arrived[k - 1, half].astype(jnp.float32)
        here = slice(half * rows, (half + 1) * rows)
        mean = (summed / scale[here]).astype(mean_rows.dtype)
        preact = own_part[here] + jnp.dot(mean, w_neigh[...], preferred_element_type=jnp.float32)
        sigmoid_values = jax.nn.sigmoid(preact)
        gradient = (
            grad_out[here].astype(jnp.float32) * sigmoid_values * (1.0 + preact * (1.0 - sigmoid_values))
        ).astype(grad_preact.dtype)
        sent_up = lax.dot_general(
            gradient, w_neigh[...], (((1,), (1,)), ((), ())), preferred_element_type=jnp.float32
        )
        upward[half] = (sent_up / scale[here]).astype(upward.dtype)
        target = upward_rows.at[col, half]
        for k in far_first:
            gathered[half, k] = start(
                upward.at[half], target, up_send, up_recv, half * (ny - 1) + k - 1, along_y[k]
            )
        passed.append(start(upward.at[half], target, pass_send, pass_recv, half * ny, sibling))
        kept.append(pltpu.make_async_copy(upward.at[half], target, keep_sem.at[half]))
        kept[-1].start()
        layer_out[here] = (preact * sigmoid_values).astype(layer_out.dtype)
        mean_rows[here] = mean
        grad_preact[here] = gradient
    for half in range(halves):
        for k in reversed(far_first):
            gathered[half, k].wait_recv()
            held = upward_rows.at[2 * lax.rem(y + ny - k, ny) + core, half]
            passed.append(start(held, held, pass_send, pass_recv, half * ny + k, sibling))
    for each in passed:
        each.wait_recv()
    for each in started:
        each.wait_send()
    for each in kept:
        each.wait()


def scatter_kernel(
    transfers, order, n_parts, nx, nz, n_col, grad_scale, partial, features, mean_rows, grad_preact, w_self,
    moved_in, weight_sums,
    total, arrived, parts, col_arrived, col_sums, z_arrived, x_sums, z_sums, all_sums,
    load_sem, send_sem, recv_sem, c_send, c_recv, z_send, z_recv, x_send, x_recv, zz_send, zz_recv, cc_send, cc_recv,
):
    torus = Torus(nx, nz)
    col = lax.axis_index("col")
    load = pltpu.make_async_copy(partial, total, load_sem)
    load.start()
    barrier = pltpu.get_barrier_semaphore()
    along_z = [{"row": torus.row(0, k)} for k in range(1, nz)]
    along_x = [{"row": torus.row(k, 0)} for k in range(1, nx)]
    cols = [lax.rem(col + k, n_col) for k in range(n_col)]
    along_col = [{"col": c} for c in cols[1:]]
    greet(barrier, along_z + along_x + along_col)
    moved = jnp.dot(
        row_order(grad_preact.shape[0]), grad_preact[...], preferred_element_type=jnp.float32
    ).astype(jnp.bfloat16)
    self_grad = lax.dot_general(
        moved, w_self[...], (((1,), (1,)), ((), ())), preferred_element_type=jnp.float32
    )
    rows = w_self.shape[0] // n_col
    for half, source in enumerate((features, mean_rows)):
        product = lax.dot_general(
            source[...], grad_preact[...], (((0,), (0,)), ((), ())), preferred_element_type=jnp.float32
        ).astype(parts.dtype)
        for c in range(n_col):
            parts[c, half * rows : (half + 1) * rows] = product[c * rows : (c + 1) * rows]
    pl.semaphore_wait(barrier, len(along_z) + len(along_x) + len(along_col))

    started = []

    def start(source, target, sends, recvs, k, peer):
        started.append(
            pltpu.make_async_remote_copy(
                src_ref=source,
                dst_ref=target,
                send_sem=sends.at[k],
                recv_sem=recvs.at[k],
                device_id=peer,
                device_id_type=MESH,
            )
        )
        started[-1].start()
        return started[-1]

    def reduce_along_col():
        return [
            start(parts.at[cols[k]], col_arrived.at[k - 1], c_send, c_recv, k - 1, peer)
            for k, peer in enumerate(along_col, 1)
        ]

    def reduce_along_z(before):
        for each in before:
            each.wait_recv()
        part = parts[col].astype(jnp.float32)
        for k in range(n_col - 1):
            part = part + col_arrived[k].astype(jnp.float32)
        col_sums[...] = part.reshape(col_sums.shape)
        return [
            start(col_sums.at[lax.rem(torus.z + k, nz)], z_arrived.at[k - 1], z_send, z_recv, k - 1, peer)
            for k, peer in enumerate(along_z, 1)
        ]

    def reduce_along_x(before):
        for each in before:
            each.wait_recv()
        part = col_sums[torus.z]
        for k in range(nz - 1):
            part = part + z_arrived[k]
        x_sums[torus.x] = part
        return [
            start(x_sums.at[torus.x], x_sums.at[torus.x], x_send, x_recv, k, peer)
            for k, peer in enumerate(along_x)
        ]

    def gather_along_z(before):
        for each in before:
            each.wait_recv()
        part = x_sums[0]
        for k in range(1, nx):
            part = part + x_sums[k]
        z_sums[torus.z] = part * grad_scale
        return [
            start(z_sums.at[torus.z], z_sums.at[torus.z], zz_send, zz_recv, k, peer)
            for k, peer in enumerate(along_z)
        ]

    def gather_along_col(before):
        for each in before:
            each.wait_recv()
        all_sums[col] = z_sums[...].reshape(all_sums.shape[1:])
        return [
            start(all_sums.at[col], all_sums.at[col], cc_send, cc_recv, k, peer)
            for k, peer in enumerate(along_col)
        ]

    def copy(index, node):
        axis, sign, first, count, _ = transfers[index]
        return start(
            total.at[torus.row(node[1], node[2]), pl.ds(first, count)],
            arrived.at[index, pl.ds(0, count)],
            send_sem,
            recv_sem,
            index,
            torus.neighbour(axis, -sign),
        )

    sent = {}
    pending = reduce_along_col()
    steps = (reduce_along_z, reduce_along_x, gather_along_z, gather_along_col)
    stages = {len(order) * (k + 2) // 7: step for k, step in enumerate(steps)}
    load.wait()
    for position, (node, brought, carried) in enumerate(reversed(order)):
        if position in stages:
            pending = stages[position](pending)
        owner = torus.row(node[1], node[2])
        for index in reversed(carried):
            first, count = transfers[index][2:4]
            sent[index].wait_recv()
            if brought:
                rows = pl.ds(first, count)
                total[owner, rows] = (
                    total[owner, rows].astype(jnp.float32)
                    + arrived[index, :count].astype(jnp.float32)
                ).astype(total.dtype)
        for index in reversed(brought):
            sent[index] = copy(index, node)

    me = torus.row(0, 0)
    sums = []
    for (node, _, first_carried), (_, _, carried) in zip(order[:n_parts], order[n_parts:]):
        carried = first_carried + carried
        first = min(transfers[index][2] for index in carried)
        full = max(transfers[index][2] + transfers[index][3] for index in carried) - first
        part = total[me, first : first + full].astype(jnp.float32)
        for index in carried:
            lead, count = transfers[index][2:4]
            came = arrived[index, :count].astype(jnp.float32)
            if count < full:
                filler = jnp.zeros((full - count, came.shape[1]), jnp.float32)
                came = jnp.concatenate([came, filler] if lead == first else [filler, came], axis=0)
            part = part + came
        sums.append((first, part))
    neighbour_sum = jnp.concatenate([part for _, part in sorted(sums, key=lambda pair: pair[0])], axis=0)
    moved_in[...] = (self_grad + neighbour_sum).astype(moved_in.dtype)
    for each in pending:
        each.wait_recv()
    weight_sums[...] = all_sums[...]
    for each in started:
        each.wait_send()


def finish_kernel(moved_in, weight_sums, grad_in, grad_self, grad_neigh):
    grad_in[...] = lax.dot_general(
        row_order(moved_in.shape[0]), moved_in[...], (((0,), (0,)), ((), ())), preferred_element_type=jnp.float32
    ).astype(grad_in.dtype)
    rows = weight_sums.shape[1] // 2
    for c in range(weight_sums.shape[0]):
        grad_self[c * rows : (c + 1) * rows] = weight_sums[c, :rows]
        grad_neigh[c * rows : (c + 1) * rows] = weight_sums[c, rows:]


def shards(features, grad_out, degrees, w_self, w_neigh, bias, tile_slots, tile_count, tile_masks):
    size, width = features.shape
    n_row, n_col = lax.axis_size("row"), lax.axis_size("col")
    nx, nz = 4, n_row // 4
    split = [("xz", 0, 48), ("xz", 48, 48), ("zx", 96, 80), ("zx", 176, 80)]
    transfers, order = torus_plan(nx, nz, split)
    copies = len(transfers)
    bf16, f32 = jnp.bfloat16, jnp.float32
    dma = pltpu.SemaphoreType.DMA
    slots, count, masks = tile_slots[0, 0], tile_count[0], tile_masks[0, 0]
    block_rows = size * n_col // TILE
    block_columns = size * n_row // TILE
    halves = size // TILE
    ny = n_col // 2

    def array(dtype, *shape):
        return jax.ShapeDtypeStruct(shape, dtype)

    def local(mib):
        return pltpu.CompilerParams(vmem_limit_bytes=mib << 20)

    def remote(identity, mib):
        return pltpu.CompilerParams(
            collective_id=identity, has_side_effects=True, vmem_limit_bytes=mib << 20
        )

    panel = pl.pallas_call(
        functools.partial(gather_kernel, transfers, order, nx, nz),
        name="gather_panel",
        out_shape=array(bf16, n_row, size, width),
        in_specs=[VMEM],
        out_specs=ANY,
        scratch_shapes=[pltpu.VMEM((size, width), bf16), dma, dma((copies,)), dma((copies,))],
        compiler_params=remote(0, 4),
    )(features)

    partial = pl.pallas_call(
        aggregate_kernel,
        name="aggregate",
        out_shape=array(bf16, block_rows, TILE, width),
        in_specs=[SMEM, SMEM, VMEM, VMEM],
        out_specs=VMEM,
        scratch_shapes=[pltpu.VMEM((block_rows, TILE, width), f32)],
        compiler_params=local(16),
    )(slots, count, masks, panel.reshape(block_columns, TILE, width))

    layer_in, mean_rows, grad_preact, upward_rows = pl.pallas_call(
        middle_kernel,
        name="middle",
        out_shape=(
            array(bf16, size, width),
            array(bf16, size, width),
            array(bf16, size, width),
            array(bf16, n_col, halves, TILE, width),
        ),
        in_specs=[VMEM] * 7,
        out_specs=(VMEM, VMEM, VMEM, ANY),
        scratch_shapes=[
            pltpu.VMEM((size, width), f32),
            pltpu.VMEM((size, width), f32),
            pltpu.VMEM((ny, halves, TILE, width), bf16),
            pltpu.VMEM((ny - 1, halves, TILE, width), bf16),
            pltpu.VMEM((ny - 1, halves, TILE, width), bf16),
            pltpu.VMEM((halves, TILE, width), f32),
            pltpu.VMEM((halves, TILE, width), bf16),
            dma((halves,)),
        ]
        + [dma((ny * halves,))] * 2
        + [dma(((ny - 1) * halves,))] * 4
        + [dma((ny * halves,))] * 2,
        compiler_params=remote(1, 16),
    )(
        partial.reshape(n_col, halves, TILE, width),
        features,
        grad_out,
        degrees[None, :],
        w_self,
        w_neigh,
        bias[None, :],
    )

    spread, layer_out = pl.pallas_call(
        spread_kernel,
        name="spread",
        out_shape=(array(bf16, block_columns, TILE, width), array(bf16, size, width)),
        in_specs=[SMEM, SMEM, VMEM, VMEM, ANY],
        out_specs=(VMEM, ANY),
        scratch_shapes=[pltpu.VMEM((block_columns, TILE, width), f32), dma],
        compiler_params=local(24),
    )(slots, count, masks, upward_rows.reshape(block_rows, TILE, width), layer_in)

    grad_scale = 1.0 / math.sqrt(size * n_row * n_col)
    grad_rows = 2 * width // n_col
    z_rows = grad_rows // nz
    others = n_col - 1
    moved_in, weight_sums = pl.pallas_call(
        functools.partial(scatter_kernel, transfers, order, len(split), nx, nz, n_col, grad_scale),
        name="scatter_panel",
        out_shape=(array(bf16, size, width), array(f32, n_col, grad_rows, width)),
        in_specs=[ANY, VMEM, VMEM, VMEM, VMEM],
        out_specs=(VMEM, VMEM),
        scratch_shapes=[
            pltpu.VMEM((n_row, size, width), bf16),
            pltpu.VMEM((copies, max(part[2] for part in split), width), bf16),
            pltpu.VMEM((n_col, grad_rows, width), bf16),
            pltpu.VMEM((others, grad_rows, width), bf16),
            pltpu.VMEM((nz, z_rows, width), f32),
            pltpu.VMEM((nz - 1, z_rows, width), f32),
            pltpu.VMEM((nx, z_rows, width), f32),
            pltpu.VMEM((nz, z_rows, width), f32),
            pltpu.VMEM((n_col, grad_rows, width), f32),
            dma,
            dma((copies,)),
            dma((copies,)),
        ]
        + [dma((others,))] * 2
        + [dma((nz - 1,))] * 2
        + [dma((nx - 1,))] * 2
        + [dma((nz - 1,))] * 2
        + [dma((others,))] * 2,
        compiler_params=remote(2, 24),
    )(spread.reshape(n_row, size, width), features, mean_rows, grad_preact, w_self)

    grad_in, grad_self, grad_neigh = pl.pallas_call(
        finish_kernel,
        name="finish",
        out_shape=(array(bf16, size, width), array(f32, width, width), array(f32, width, width)),
        in_specs=[VMEM, VMEM],
        out_specs=(VMEM, VMEM, VMEM),
        compiler_params=local(8),
    )(moved_in, weight_sums)
    return (layer_out, grad_in, grad_self, grad_neigh)


def solution(mesh):
    placed = (
        P(("row", "col"), None),
        P(("row", "col"), None),
        P(("row", "col")),
        P(),
        P(),
        P(),
        P("row", "col", None),
        P("row", "col"),
        P("row", "col", None, None, None),
    )
    return jax.shard_map(
        shards,
        mesh=mesh,
        in_specs=placed,
        out_specs=(P(("row", "col"), None), P(("row", "col"), None), P(), P()),
        check_vma=False,
    )
```

```python
import functools
import heapq
import math

import jax
import jax.numpy as jnp
from jax import lax
from jax.experimental import pallas as pl
from jax.experimental.pallas import tpu as pltpu
from jax.sharding import PartitionSpec as P

MESH = pl.DeviceIdType.MESH
SMEM = pl.BlockSpec(memory_space=pltpu.SMEM)
VMEM = pl.BlockSpec(memory_space=pltpu.VMEM)
ANY = pl.BlockSpec(memory_space=pl.ANY)
TILE = 128
UNROLL = 16
STAGES = (0, 4, 9, 30, 48, 68)


def torus_plan(nx, nz, split, latency=3.0, rate=0.0085):
    size = {"x": nx, "z": nz}
    transfers, order = [], []
    free, heap = {}, []

    def wrap(d, n):
        d %= n
        return d - n if d > n // 2 else d

    def send(now, node, axis, sign, first, count):
        offset = {"x": node[1], "z": node[2]}
        offset[axis] = wrap(offset[axis] - sign, size[axis])
        index = len(transfers)
        transfers.append((axis, sign, first, count, (node[0], offset["x"], offset["z"])))
        start = max(now, free.get((axis, sign), 0.0))
        free[axis, sign] = start + count * rate
        heapq.heappush(heap, (free[axis, sign] + latency, index))
        entries[node][1].append(index)

    def forward(now, node, phases="pq"):
        part = node[0]
        (p, q), begin, full = split[part]
        offset = {"x": node[1], "z": node[2]}
        dp, dq = offset[p], offset[q]
        half_p, half_q = size[p] // 2, size[q] // 2
        lower = (full // 2 + 15) // 16 * 16
        for sign in (1, -1) if "p" in phases else ():
            if dq == 0 and (dp == 0 or -dp * sign > 0) and dp != half_p:
                if abs(dp) + 1 < half_p:
                    send(now, node, p, sign, begin, full)
                elif sign == 1:
                    send(now, node, p, sign, begin, lower)
                else:
                    send(now, node, p, sign, begin + lower, full - lower)
        for sign in (1, -1) if "q" in phases else ():
            if (dq == 0 or -dq * sign > 0) and dq != half_q:
                if abs(dq) + 1 < half_q or (0 <= dp < half_p) == (sign == 1):
                    send(now, node, q, sign, begin, full)

    got = {}
    entries = {(part, 0, 0): ([], []) for part in range(len(split))}
    roots = []
    for phases in "pq":
        for part in range(len(split)):
            forward(0.0, (part, 0, 0), phases)
            roots.append(((part, 0, 0), [], entries[part, 0, 0][1]))
            entries[part, 0, 0] = ([], [])
    while heap:
        now, index = heapq.heappop(heap)
        count, node = transfers[index][3:]
        entries.setdefault(node, ([], []))[0].append(index)
        got[node] = got.get(node, 0) + count
        if got[node] == split[node[0]][2]:
            order.append(node)
            forward(now, node)
    return transfers, roots + [(node, *entries[node]) for node in order]


class Torus:
    def __init__(self, nx, nz):
        self.nx, self.nz = nx, nz
        row = lax.axis_index("row")
        self.x, self.z = lax.rem(row, nx), lax.div(row, nx)

    def row(self, dx, dz):
        x = lax.rem(self.x + (dx + self.nx), self.nx)
        z = lax.rem(self.z + (dz + self.nz), self.nz)
        return z * self.nx + x

    def neighbour(self, axis, sign):
        return {"row": self.row(sign, 0) if axis == "x" else self.row(0, sign)}


def greet(barrier, peers):
    for peer in peers:
        pl.semaphore_signal(barrier, inc=1, device_id=peer, device_id_type=MESH)


def row_order(size):
    place = lax.broadcasted_iota(jnp.int32, (size, size), 0)
    node = lax.broadcasted_iota(jnp.int32, (size, size), 1)
    within = place & (TILE - 1)
    source = (place - within) + ((within & 15) << 3) + (within >> 4)
    return jnp.where(source == node, 1.0, 0.0).astype(jnp.bfloat16)


def gather_kernel(transfers, order, nx, nz, features, panel, own, local_sem, send_sem, recv_sem):
    torus = Torus(nx, nz)
    me = torus.row(0, 0)
    barrier = pltpu.get_barrier_semaphore()
    around = [torus.neighbour(axis, sign) for axis in "xz" for sign in (1, -1)]
    greet(barrier, around)
    own[...] = jnp.dot(
        row_order(own.shape[0]), features[...], preferred_element_type=jnp.float32
    ).astype(own.dtype)
    pl.semaphore_wait(barrier, len(around))

    def copy(index, node, source):
        axis, sign, first, count, _ = transfers[index]
        origin = torus.row(node[1], node[2])
        rows = pl.ds(first, count)
        return pltpu.make_async_remote_copy(
            src_ref=own.at[rows] if source else panel.at[origin, rows],
            dst_ref=panel.at[origin, rows],
            send_sem=send_sem.at[index],
            recv_sem=recv_sem.at[index],
            device_id=torus.neighbour(axis, sign),
            device_id_type=MESH,
        )

    keep = pltpu.make_async_copy(own, panel.at[me], local_sem)
    keep.start()
    started = []
    for node, brought, carried in order:
        for index in brought:
            copy(index, node, False).wait_recv()
        for index in carried:
            started.append(copy(index, node, not brought))
            started[-1].start()
    for each in started:
        each.wait_send()
    keep.wait()


def unpack(words):
    return jnp.concatenate(
        [((words >> bit) & 1).astype(jnp.float32).astype(jnp.bfloat16) for bit in range(8)], axis=0
    )


def each_tile(slots, live, masks, block_rows, step):
    last = masks.shape[0] - 1

    def group(index, _):
        for u in range(UNROLL):
            tile = index * UNROLL + u
            held = jnp.minimum(tile, last)
            slot = slots[held]
            words = jnp.where(tile < live, masks[held], 0)
            step(lax.rem(slot, block_rows), lax.div(slot, block_rows), unpack(words))
        return 0

    lax.fori_loop(0, lax.div(live + (UNROLL - 1), UNROLL), group, 0)


def set_zero(total):
    def one(i, _):
        total[i] = jnp.zeros(total.shape[1:], total.dtype)
        return 0

    lax.fori_loop(0, total.shape[0], one, 0)


def round_to(out, total):
    def one(i, _):
        out[i] = total[i].astype(out.dtype)
        return 0

    lax.fori_loop(0, total.shape[0], one, 0)


def aggregate_kernel(slots, count, masks, panel, out, total):
    set_zero(total)

    def step(row_block, column_block, bits):
        total[row_block] += lax.dot_general(
            bits, panel[column_block], (((0,), (0,)), ((), ())), preferred_element_type=jnp.float32
        )

    each_tile(slots, count[0], masks, out.shape[0], step)
    round_to(out, total)


def spread_kernel(slots, count, masks, upward, layer_in, out, layer_out, total, layer_sem):
    hand_on = pltpu.make_async_copy(layer_in, layer_out, layer_sem)
    hand_on.start()
    set_zero(total)

    def step(row_block, column_block, bits):
        total[column_block] += jnp.dot(bits, upward[row_block], preferred_element_type=jnp.float32)

    each_tile(slots, count[0], masks, upward.shape[0], step)
    round_to(out, total)
    hand_on.wait()


def middle_kernel(
    partial, features, grad_out, degrees, w_self, w_neigh, bias,
    layer_out, grad_preact, upward_rows, weight_sums,
    own_part, scale, from_sibling, joined, arrived, own_sum, upward, mean_rows, parts, parts_arrived,
    keep_sem, sibling_send, sibling_recv, y_send, y_recv, up_send, up_recv, pass_send, pass_recv, w_send, w_recv,
):
    col = lax.axis_index("col")
    y, core = lax.div(col, 2), lax.rem(col, 2)
    ny = partial.shape[0] // 2
    halves, rows = partial.shape[1:3]
    place = [lax.rem(y + k, ny) for k in range(ny)]
    far_first = sorted(range(1, ny), key=lambda k: -min(k, ny - k))
    sibling = {"col": 2 * y + 1 - core}
    along_y = [{"col": 2 * place[k] + core} for k in range(ny)]
    barrier = pltpu.get_barrier_semaphore()
    n_col = partial.shape[0]
    along_col = [{"col": lax.rem(col + k, n_col)} for k in range(1, n_col)]
    greet(barrier, along_col)
    size, width = features.shape
    scale[...] = jnp.broadcast_to(degrees[...].astype(jnp.float32), (width, size)).T
    own_part[...] = bias[...] + jnp.dot(
        features[...], w_self[...], preferred_element_type=jnp.float32
    )
    pl.semaphore_wait(barrier, n_col - 1)

    started = []

    def start(source, target, sends, recvs, k, peer):
        copy = pltpu.make_async_remote_copy(
            src_ref=source,
            dst_ref=target,
            send_sem=sends.at[k],
            recv_sem=recvs.at[k],
            device_id=peer,
            device_id_type=MESH,
        )
        copy.start()
        started.append(copy)
        return copy

    pieces = [(half, k) for half in range(halves) for k in (*far_first, 0)]
    shared = {}
    for half, k in pieces:
        shared[half, k] = start(
            partial.at[2 * place[k] + 1 - core, half], from_sibling.at[k, half],
            sibling_send, sibling_recv, half * ny + k, sibling,
        )
    exchanged = {}
    for half, k in pieces:
        shared[half, k].wait_recv()
        both = partial[2 * place[k] + core, half].astype(jnp.float32)
        both = both + from_sibling[k, half].astype(jnp.float32)
        if k == 0:
            own_sum[half] = both
        else:
            joined[k - 1, half] = both.astype(joined.dtype)
            exchanged[half, k] = start(
                joined.at[k - 1, half], arrived.at[k - 1, half],
                y_send, y_recv, half * (ny - 1) + k - 1, along_y[k],
            )
    gathered, passed, kept = {}, [], []
    for half in range(halves):
        summed = own_sum[half]
        for k in far_first:
            exchanged[half, k].wait_recv()
            summed = summed + arrived[k - 1, half].astype(jnp.float32)
        here = slice(half * rows, (half + 1) * rows)
        mean = (summed / scale[here]).astype(mean_rows.dtype)
        preact = own_part[here] + jnp.dot(mean, w_neigh[...], preferred_element_type=jnp.float32)
        sigmoid_values = jax.nn.sigmoid(preact)
        gradient = (
            grad_out[here].astype(jnp.float32) * sigmoid_values * (1.0 + preact * (1.0 - sigmoid_values))
        ).astype(grad_preact.dtype)
        sent_up = lax.dot_general(
            gradient, w_neigh[...], (((1,), (1,)), ((), ())), preferred_element_type=jnp.float32
        )
        upward[half] = (sent_up / scale[here]).astype(upward.dtype)
        target = upward_rows.at[col, half]
        for k in far_first:
            gathered[half, k] = start(
                upward.at[half], target, up_send, up_recv, half * (ny - 1) + k - 1, along_y[k]
            )
        passed.append(start(upward.at[half], target, pass_send, pass_recv, half * ny, sibling))
        kept.append(pltpu.make_async_copy(upward.at[half], target, keep_sem.at[half]))
        kept[-1].start()
        layer_out[here] = (preact * sigmoid_values).astype(layer_out.dtype)
        mean_rows[here] = mean
        grad_preact[here] = gradient
    part_rows = width // n_col
    for which, source in enumerate((features, mean_rows)):
        product = lax.dot_general(
            source[...], grad_preact[...], (((0,), (0,)), ((), ())), preferred_element_type=jnp.float32
        ).astype(parts.dtype)
        for c in range(n_col):
            parts[c, which * part_rows : (which + 1) * part_rows] = product[
                c * part_rows : (c + 1) * part_rows
            ]
    reduced = [
        start(parts.at[lax.rem(col + k, n_col)], parts_arrived.at[k - 1], w_send, w_recv, k - 1, peer)
        for k, peer in enumerate(along_col, 1)
    ]
    for half in range(halves):
        for k in reversed(far_first):
            gathered[half, k].wait_recv()
            held = upward_rows.at[2 * lax.rem(y + ny - k, ny) + core, half]
            passed.append(start(held, held, pass_send, pass_recv, half * ny + k, sibling))
    total = parts[col].astype(jnp.float32)
    for k, each in enumerate(reduced):
        each.wait_recv()
        total = total + parts_arrived[k].astype(jnp.float32)
    weight_sums[...] = total
    for each in passed:
        each.wait_recv()
    for each in started:
        each.wait_send()
    for each in kept:
        each.wait()


def scatter_kernel(
    transfers, order, split, nx, nz, n_col, grad_scale, partial, weight_parts, grad_preact, w_self,
    moved_in, weight_sums,
    arrived, self_grad, z_arrived, x_sums, z_sums,
    news, send_sem, recv_sem, z_send, z_recv, x_send, x_recv, zz_send, zz_recv, cc_send, cc_recv,
):
    torus = Torus(nx, nz)
    col = lax.axis_index("col")
    cols = [lax.rem(col + k, n_col) for k in range(n_col)]
    along_col = [{"col": c} for c in cols[1:]]
    along_z = [{"row": torus.row(0, k)} for k in range(1, nz)]
    along_x = [{"row": torus.row(k, 0)} for k in range(1, nx)]
    z_next, x_next = [along_z[0], along_z[-1]], [along_x[0], along_x[-1]]
    y_next = [{"col": cols[2]}, {"col": cols[-2]}]
    sibling = {"col": col + 1 - 2 * lax.rem(col, 2)}
    barrier = pltpu.get_barrier_semaphore()
    greet(barrier, [*z_next, *x_next, *y_next, sibling])
    rounds = [[*z_next, *x_next, *y_next], [*z_next, *y_next], z_next]

    def tell(number):
        greet(news.at[number], rounds[number])

    def hear(number):
        pl.semaphore_wait(news.at[number], len(rounds[number]))

    pl.semaphore_wait(barrier, 7)
    tell(0)

    started = []

    def start(source, target, sends, recvs, k, peer):
        started.append(
            pltpu.make_async_remote_copy(
                src_ref=source,
                dst_ref=target,
                send_sem=sends.at[k],
                recv_sem=recvs.at[k],
                device_id=peer,
                device_id_type=MESH,
            )
        )
        started[-1].start()
        return started[-1]

    def pass_first(_):
        hear(0)
        tell(1)
        moved = jnp.dot(
            row_order(grad_preact.shape[0]), grad_preact[...], preferred_element_type=jnp.float32
        ).astype(jnp.bfloat16)
        self_grad[...] = lax.dot_general(
            moved, w_self[...], (((1,), (1,)), ((), ())), preferred_element_type=jnp.float32
        )

    def pass_second(_):
        hear(1)
        tell(2)

    def reduce_along_z(_):
        hear(2)
        return [
            start(weight_parts.at[lax.rem(torus.z + k, nz)], z_arrived.at[k - 1], z_send, z_recv, k - 1, peer)
            for k, peer in enumerate(along_z, 1)
        ]

    def reduce_along_x(before):
        for each in before:
            each.wait_recv()
        part = weight_parts[torus.z]
        for k in range(nz - 1):
            part = part + z_arrived[k]
        x_sums[torus.x] = part
        return [
            start(x_sums.at[torus.x], x_sums.at[torus.x], x_send, x_recv, k, peer)
            for k, peer in enumerate(along_x)
        ]

    def gather_along_z(before):
        for each in before:
            each.wait_recv()
        part = x_sums[0]
        for k in range(1, nx):
            part = part + x_sums[k]
        z_sums[torus.z] = part * grad_scale
        return [
            start(z_sums.at[torus.z], z_sums.at[torus.z], zz_send, zz_recv, k, peer)
            for k, peer in enumerate(along_z)
        ]

    def gather_along_col(before):
        for each in before:
            each.wait_recv()
        weight_sums[col] = z_sums[...].reshape(weight_sums.shape[1:]).astype(weight_sums.dtype)
        return [
            start(weight_sums.at[col], weight_sums.at[col], cc_send, cc_recv, k, peer)
            for k, peer in enumerate(along_col)
        ]

    def carry(index, source):
        axis, sign, _, count, _ = transfers[index]
        return start(
            source,
            arrived.at[index, pl.ds(0, count)],
            send_sem,
            recv_sem,
            index,
            torus.neighbour(axis, -sign),
        )

    def sum_of(node, carried):
        _, first, full = split[node[0]]
        value = partial[torus.row(node[1], node[2]), first : first + full].astype(jnp.float32)
        for index in reversed(carried):
            lead, count = transfers[index][2:4]
            sent[index].wait_recv()
            came = arrived[index, :count].astype(jnp.float32)
            if count < full:
                filler = jnp.zeros((full - count, came.shape[1]), jnp.float32)
                came = jnp.concatenate([came, filler] if lead == first else [filler, came], axis=0)
            value = value + came
        return value

    sent = {}
    pending = []
    steps = [pass_first, pass_second, reduce_along_z, reduce_along_x, gather_along_z, gather_along_col]
    n_parts = len(split)
    inner = sum(1 for _, brought, carried in order if brought and carried)
    stages = {inner * at // 100: step for at, step in zip(STAGES, steps)}
    seen = 0
    for node, brought, carried in reversed(order[2 * n_parts :]):
        begin = split[node[0]][1]
        if carried:
            if seen in stages:
                pending = stages[seen](pending)
            seen += 1
            full = split[node[0]][2]
            home = next(index for index in carried if transfers[index][3] == full)
            if len(carried) == 1:
                sent[home].wait_recv()
                arrived[home, :full] += partial[torus.row(node[1], node[2]), begin : begin + full]
            else:
                arrived[home, :full] = sum_of(node, carried).astype(arrived.dtype)
        for index in reversed(brought):
            first, count = transfers[index][2:4]
            if carried:
                source = arrived.at[home, pl.ds(first - begin, count)]
            else:
                source = partial.at[torus.row(node[1], node[2]), pl.ds(first, count)]
            sent[index] = carry(index, source)

    sums = []
    for (node, _, first_carried), (_, _, carried) in zip(order[:n_parts], order[n_parts:]):
        sums.append((split[node[0]][1], sum_of(node, first_carried + carried)))
    neighbour_sum = jnp.concatenate([part for _, part in sorted(sums, key=lambda pair: pair[0])], axis=0)
    moved_in[...] = (self_grad[...] + neighbour_sum).astype(moved_in.dtype)
    for each in pending:
        each.wait_recv()
    for each in started:
        each.wait_send()


def finish_kernel(moved_in, weight_sums, grad_in, grad_self, grad_neigh):
    grad_in[...] = lax.dot_general(
        row_order(moved_in.shape[0]), moved_in[...], (((0,), (0,)), ((), ())), preferred_element_type=jnp.float32
    ).astype(grad_in.dtype)
    rows = weight_sums.shape[1] // 2
    for c in range(weight_sums.shape[0]):
        grad_self[c * rows : (c + 1) * rows] = weight_sums[c, :rows].astype(grad_self.dtype)
        grad_neigh[c * rows : (c + 1) * rows] = weight_sums[c, rows:].astype(grad_neigh.dtype)


def array(dtype, *shape):
    return jax.ShapeDtypeStruct(shape, dtype)


def local(mib):
    return pltpu.CompilerParams(vmem_limit_bytes=mib << 20)


def remote(identity, mib):
    return pltpu.CompilerParams(
        collective_id=identity, has_side_effects=True, vmem_limit_bytes=mib << 20
    )


def gather_panel(features, nx, nz, split, identity=0):
    size, width = features.shape
    transfers, order = torus_plan(nx, nz, split)
    copies = len(transfers)
    return pl.pallas_call(
        functools.partial(gather_kernel, transfers, order, nx, nz),
        name="gather_panel",
        out_shape=array(jnp.bfloat16, nx * nz, size, width),
        in_specs=[VMEM],
        out_specs=ANY,
        scratch_shapes=[
            pltpu.VMEM((size, width), jnp.bfloat16),
            pltpu.SemaphoreType.DMA,
            pltpu.SemaphoreType.DMA((copies,)),
            pltpu.SemaphoreType.DMA((copies,)),
        ],
        compiler_params=remote(identity, 4),
    )(features)


def middle(partial, features, grad_out, degrees, w_self, w_neigh, bias, identity=1):
    bf16, f32 = jnp.bfloat16, jnp.float32
    dma = pltpu.SemaphoreType.DMA
    size, width = features.shape
    n_col, halves = partial.shape[:2]
    ny = n_col // 2
    return pl.pallas_call(
        middle_kernel,
        name="middle",
        out_shape=(
            array(bf16, size, width),
            array(bf16, size, width),
            array(bf16, n_col, halves, TILE, width),
            array(f32, 2 * width // n_col, width),
        ),
        in_specs=[VMEM] * 7,
        out_specs=(VMEM, VMEM, ANY, VMEM),
        scratch_shapes=[
            pltpu.VMEM((size, width), f32),
            pltpu.VMEM((size, width), f32),
            pltpu.VMEM((ny, halves, TILE, width), bf16),
            pltpu.VMEM((ny - 1, halves, TILE, width), bf16),
            pltpu.VMEM((ny - 1, halves, TILE, width), bf16),
            pltpu.VMEM((halves, TILE, width), f32),
            pltpu.VMEM((halves, TILE, width), bf16),
            pltpu.VMEM((size, width), bf16),
            pltpu.VMEM((n_col, 2 * width // n_col, width), bf16),
            pltpu.VMEM((n_col - 1, 2 * width // n_col, width), bf16),
            dma((halves,)),
        ]
        + [dma((ny * halves,))] * 2
        + [dma(((ny - 1) * halves,))] * 4
        + [dma((ny * halves,))] * 2
        + [dma((n_col - 1,))] * 2,
        compiler_params=remote(identity, 16),
    )(
        partial,
        features,
        grad_out,
        degrees[None, :],
        w_self,
        w_neigh,
        bias[None, :],
    )


def scatter_panel(spread, weight_parts, grad_preact, w_self, nx, nz, n_col, split, identity=2):
    bf16, f32 = jnp.bfloat16, jnp.float32
    dma = pltpu.SemaphoreType.DMA
    size, width = grad_preact.shape
    transfers, order = torus_plan(nx, nz, split)
    copies = len(transfers)
    grad_scale = 1.0 / math.sqrt(size * nx * nz * n_col)
    grad_rows = 2 * width // n_col
    z_rows = grad_rows // nz
    others = n_col - 1
    return pl.pallas_call(
        functools.partial(scatter_kernel, transfers, order, split, nx, nz, n_col, grad_scale),
        name="scatter_panel",
        out_shape=(array(bf16, size, width), array(bf16, n_col, grad_rows, width)),
        in_specs=[VMEM, VMEM, VMEM, VMEM],
        out_specs=(VMEM, VMEM),
        scratch_shapes=[
            pltpu.VMEM((copies, max(part[2] for part in split), width), bf16),
            pltpu.VMEM((size, width), f32),
            pltpu.VMEM((nz - 1, z_rows, width), f32),
            pltpu.VMEM((nx, z_rows, width), f32),
            pltpu.VMEM((nz, z_rows, width), f32),
            pltpu.SemaphoreType.REGULAR((3,)),
            dma((copies,)),
            dma((copies,)),
        ]
        + [dma((nz - 1,))] * 2
        + [dma((nx - 1,))] * 2
        + [dma((nz - 1,))] * 2
        + [dma((others,))] * 2,
        compiler_params=remote(identity, 24),
    )(spread, weight_parts.reshape(nz, z_rows, width), grad_preact, w_self)


def shards(features, grad_out, degrees, w_self, w_neigh, bias, tile_slots, tile_count, tile_masks):
    size, width = features.shape
    n_row, n_col = lax.axis_size("row"), lax.axis_size("col")
    nx, nz = 4, n_row // 4
    split = [("xz", 0, 48), ("xz", 48, 48), ("zx", 96, 80), ("zx", 176, 80)]
    bf16, f32 = jnp.bfloat16, jnp.float32
    dma = pltpu.SemaphoreType.DMA
    slots, count, masks = tile_slots[0, 0], tile_count[0], tile_masks[0, 0]
    block_rows = size * n_col // TILE
    block_columns = size * n_row // TILE
    halves = size // TILE

    panel = gather_panel(features, nx, nz, split)

    partial = pl.pallas_call(
        aggregate_kernel,
        name="aggregate",
        out_shape=array(bf16, block_rows, TILE, width),
        in_specs=[SMEM, SMEM, VMEM, VMEM],
        out_specs=VMEM,
        scratch_shapes=[pltpu.VMEM((block_rows, TILE, width), f32)],
        compiler_params=local(16),
    )(slots, count, masks, panel.reshape(block_columns, TILE, width))

    layer_in, grad_preact, upward_rows, weight_parts = middle(
        partial.reshape(n_col, halves, TILE, width), features, grad_out, degrees, w_self, w_neigh, bias
    )

    spread, layer_out = pl.pallas_call(
        spread_kernel,
        name="spread",
        out_shape=(array(bf16, block_columns, TILE, width), array(bf16, size, width)),
        in_specs=[SMEM, SMEM, VMEM, VMEM, ANY],
        out_specs=(VMEM, ANY),
        scratch_shapes=[pltpu.VMEM((block_columns, TILE, width), f32), dma],
        compiler_params=local(24),
    )(slots, count, masks, upward_rows.reshape(block_rows, TILE, width), layer_in)

    moved_in, weight_sums = scatter_panel(
        spread.reshape(n_row, size, width), weight_parts, grad_preact, w_self, nx, nz, n_col, split
    )

    grad_in, grad_self, grad_neigh = pl.pallas_call(
        finish_kernel,
        name="finish",
        out_shape=(array(bf16, size, width), array(f32, width, width), array(f32, width, width)),
        in_specs=[VMEM, VMEM],
        out_specs=(VMEM, VMEM, VMEM),
        compiler_params=local(8),
    )(moved_in, weight_sums)
    return (layer_out, grad_in, grad_self, grad_neigh)


def solution(mesh):
    placed = (
        P(("row", "col"), None),
        P(("row", "col"), None),
        P(("row", "col")),
        P(),
        P(),
        P(),
        P("row", "col", None),
        P("row", "col"),
        P("row", "col", None, None, None),
    )
    return jax.shard_map(
        shards,
        mesh=mesh,
        in_specs=placed,
        out_specs=(P(("row", "col"), None), P(("row", "col"), None), P(), P()),
        check_vma=False,
    )
```

```python
import functools
import heapq
import math

import jax
import jax.numpy as jnp
from jax import lax
from jax.experimental import pallas as pl
from jax.experimental.pallas import tpu as pltpu
from jax.sharding import PartitionSpec as P

MESH = pl.DeviceIdType.MESH
SMEM = pl.BlockSpec(memory_space=pltpu.SMEM)
VMEM = pl.BlockSpec(memory_space=pltpu.VMEM)
ANY = pl.BlockSpec(memory_space=pl.ANY)
TILE = 128
UNROLL = 16
STAGES = (0, 2, 18, 38, 58)


def torus_plan(nx, nz, split, latency=4.0, rate=0.0085):
    size = {"x": nx, "z": nz}
    transfers, order = [], []
    free, heap = {}, []

    def wrap(d, n):
        d %= n
        return d - n if d > n // 2 else d

    def send(now, node, axis, sign, first, count):
        offset = {"x": node[1], "z": node[2]}
        offset[axis] = wrap(offset[axis] - sign, size[axis])
        index = len(transfers)
        transfers.append((axis, sign, first, count, (node[0], offset["x"], offset["z"])))
        start = max(now, free.get((axis, sign), 0.0))
        free[axis, sign] = start + count * rate
        heapq.heappush(heap, (free[axis, sign] + latency, index))
        entries[node][1].append(index)

    def forward(now, node, phases="pq"):
        part = node[0]
        (p, q), begin, full = split[part]
        offset = {"x": node[1], "z": node[2]}
        dp, dq = offset[p], offset[q]
        half_p, half_q = size[p] // 2, size[q] // 2
        lower = (full // 2 + 15) // 16 * 16
        for sign in (1, -1) if "p" in phases else ():
            if dq == 0 and (dp == 0 or -dp * sign > 0) and dp != half_p:
                if abs(dp) + 1 < half_p:
                    send(now, node, p, sign, begin, full)
                elif sign == 1:
                    send(now, node, p, sign, begin, lower)
                else:
                    send(now, node, p, sign, begin + lower, full - lower)
        for sign in (1, -1) if "q" in phases else ():
            if (dq == 0 or -dq * sign > 0) and dq != half_q:
                if abs(dq) + 1 < half_q or (0 <= dp < half_p) == (sign == 1):
                    send(now, node, q, sign, begin, full)

    got = {}
    entries = {(part, 0, 0): ([], []) for part in range(len(split))}
    roots = []
    for phases in "pq":
        for part in range(len(split)):
            forward(0.0, (part, 0, 0), phases)
            roots.append(((part, 0, 0), [], entries[part, 0, 0][1]))
            entries[part, 0, 0] = ([], [])
    while heap:
        now, index = heapq.heappop(heap)
        count, node = transfers[index][3:]
        entries.setdefault(node, ([], []))[0].append(index)
        got[node] = got.get(node, 0) + count
        if got[node] == split[node[0]][2]:
            order.append(node)
            forward(now, node)
    return transfers, roots + [(node, *entries[node]) for node in order]


class Torus:
    def __init__(self, nx, nz):
        self.nx, self.nz = nx, nz
        row = lax.axis_index("row")
        self.x, self.z = lax.rem(row, nx), lax.div(row, nx)

    def row(self, dx, dz):
        x = lax.rem(self.x + (dx + self.nx), self.nx)
        z = lax.rem(self.z + (dz + self.nz), self.nz)
        return z * self.nx + x

    def neighbour(self, axis, sign):
        return {"row": self.row(sign, 0) if axis == "x" else self.row(0, sign)}


def greet(barrier, peers):
    for peer in peers:
        pl.semaphore_signal(barrier, inc=1, device_id=peer, device_id_type=MESH)


def row_order(size):
    place = lax.broadcasted_iota(jnp.int32, (size, size), 0)
    node = lax.broadcasted_iota(jnp.int32, (size, size), 1)
    within = place & (TILE - 1)
    source = (place - within) + ((within & 15) << 3) + (within >> 4)
    return jnp.where(source == node, 1.0, 0.0).astype(jnp.bfloat16)


class Sender:
    def __init__(self):
        self.started = []

    def __call__(self, source, target, sends, recvs, k, peer):
        copy = pltpu.make_async_remote_copy(
            src_ref=source,
            dst_ref=target,
            send_sem=sends.at[k],
            recv_sem=recvs.at[k],
            device_id=peer,
            device_id_type=MESH,
        )
        copy.start()
        self.started.append(copy)
        return copy


def gather_phase(start, torus, transfers, order, own, panel, send_sem, recv_sem, sent):
    for node, brought, carried in order:
        for index in brought:
            sent[index].wait_recv()
        origin = torus.row(node[1], node[2])
        for index in carried:
            axis, sign, first, count, _ = transfers[index]
            rows = pl.ds(first, count)
            sent[index] = start(
                panel.at[origin, rows] if brought else own.at[rows],
                panel.at[origin, rows],
                send_sem,
                recv_sem,
                index,
                torus.neighbour(axis, sign),
            )
    return sent


def unpack(words):
    return jnp.concatenate(
        [((words >> bit) & 1).astype(jnp.float32).astype(jnp.bfloat16) for bit in range(8)], axis=0
    )


def chain_tiles(slots, before, masks, sums, product):
    def group(index, _):
        for u in range(UNROLL):
            tile = index * UNROLL + u
            sums[tile + 1] = sums[before[tile]] + product(slots[tile], unpack(masks[tile]))
        return 0

    lax.fori_loop(0, masks.shape[0] // UNROLL, group, 0)


def middle_phase(
    start, col, partial, features, grad_out, w_neigh, layer_out, grad_preact, upward_rows, weight_parts,
    own_part, scale, from_sibling, joined, arrived, own_sum, upward, mean_rows, parts, parts_arrived,
    keep_sem, sibling_send, sibling_recv, y_send, y_recv, up_send, up_recv, pass_send, pass_recv, w_send, w_recv,
):
    y, core = lax.div(col, 2), lax.rem(col, 2)
    ny, halves, rows = from_sibling.shape[:3]
    n_col = 2 * ny
    width = features.shape[1]
    place = [lax.rem(y + k, ny) for k in range(ny)]
    far_first = sorted(range(1, ny), key=lambda k: -min(k, ny - k))
    sibling = {"col": 2 * y + 1 - core}
    along_y = [{"col": 2 * place[k] + core} for k in range(ny)]
    along_col = [{"col": lax.rem(col + k, n_col)} for k in range(1, n_col)]
    pieces = [(half, k) for half in range(halves) for k in (*far_first, 0)]
    shared = {}
    for half, k in pieces:
        shared[half, k] = start(
            partial.at[4 * place[k] + 2 * (1 - core) + half], from_sibling.at[k, half],
            sibling_send, sibling_recv, half * ny + k, sibling,
        )
    exchanged = {}
    for half, k in pieces:
        shared[half, k].wait_recv()
        both = partial[4 * place[k] + 2 * core + half].astype(jnp.float32)
        both = both + from_sibling[k, half].astype(jnp.float32)
        if k == 0:
            own_sum[half] = both
        else:
            joined[k - 1, half] = both.astype(joined.dtype)
            exchanged[half, k] = start(
                joined.at[k - 1, half], arrived.at[k - 1, half],
                y_send, y_recv, half * (ny - 1) + k - 1, along_y[k],
            )
    gathered, passed, kept = {}, [], []
    for half in range(halves):
        summed = own_sum[half]
        for k in far_first:
            exchanged[half, k].wait_recv()
            summed = summed + arrived[k - 1, half].astype(jnp.float32)
        here = slice(half * rows, (half + 1) * rows)
        mean = (summed / scale[here]).astype(mean_rows.dtype)
        preact = own_part[here] + jnp.dot(mean, w_neigh[...], preferred_element_type=jnp.float32)
        sigmoid_values = jax.nn.sigmoid(preact)
        gradient = (
            grad_out[here].astype(jnp.float32) * sigmoid_values * (1.0 + preact * (1.0 - sigmoid_values))
        ).astype(grad_preact.dtype)
        sent_up = lax.dot_general(
            gradient, w_neigh[...], (((1,), (1,)), ((), ())), preferred_element_type=jnp.float32
        )
        upward[half] = (sent_up / scale[here]).astype(upward.dtype)
        target = upward_rows.at[2 * col + half]
        for k in far_first:
            gathered[half, k] = start(
                upward.at[half], target, up_send, up_recv, half * (ny - 1) + k - 1, along_y[k]
            )
        passed.append(start(upward.at[half], target, pass_send, pass_recv, half * ny, sibling))
        kept.append(pltpu.make_async_copy(upward.at[half], target, keep_sem.at[half]))
        kept[-1].start()
        layer_out[here] = (preact * sigmoid_values).astype(layer_out.dtype)
        mean_rows[here] = mean
        grad_preact[here] = gradient
    part_rows = width // n_col
    for which, source in enumerate((features, mean_rows)):
        product = lax.dot_general(
            source[...], grad_preact[...], (((0,), (0,)), ((), ())), preferred_element_type=jnp.float32
        ).astype(parts.dtype)
        for c in range(n_col):
            parts[c, which * part_rows : (which + 1) * part_rows] = product[
                c * part_rows : (c + 1) * part_rows
            ]
    reduced = [
        start(parts.at[lax.rem(col + k, n_col)], parts_arrived.at[k - 1], w_send, w_recv, k - 1, peer)
        for k, peer in enumerate(along_col, 1)
    ]
    for half in range(halves):
        for k in reversed(far_first):
            gathered[half, k].wait_recv()
            held = upward_rows.at[4 * lax.rem(y + ny - k, ny) + 2 * core + half]
            passed.append(start(held, held, pass_send, pass_recv, half * ny + k, sibling))
    total = parts[col].astype(jnp.float32)
    for k, each in enumerate(reduced):
        each.wait_recv()
        total = total + parts_arrived[k].astype(jnp.float32)
    weight_parts[...] = total.reshape(weight_parts.shape)
    for each in passed:
        each.wait_recv()
    for each in kept:
        each.wait()


def scatter_phase(
    start, torus, col, transfers, order, split, n_col, grad_scale, partial, weight_parts, grad_preact, w_self,
    moved_in, weight_sums, arrived, self_grad, z_arrived, x_sums, z_sums,
    send_sem, recv_sem, z_send, z_recv, x_send, x_recv, zz_send, zz_recv, cc_send, cc_recv,
):
    nx, nz = torus.nx, torus.nz
    along_col = [{"col": lax.rem(col + k, n_col)} for k in range(1, n_col)]
    along_z = [{"row": torus.row(0, k)} for k in range(1, nz)]
    along_x = [{"row": torus.row(k, 0)} for k in range(1, nx)]

    def multiply_self(before):
        moved = jnp.dot(
            row_order(grad_preact.shape[0]), grad_preact[...], preferred_element_type=jnp.float32
        ).astype(jnp.bfloat16)
        self_grad[...] = lax.dot_general(
            moved, w_self[...], (((1,), (1,)), ((), ())), preferred_element_type=jnp.float32
        )
        return before

    def reduce_along_z(_):
        return [
            start(weight_parts.at[lax.rem(torus.z + k, nz)], z_arrived.at[k - 1], z_send, z_recv, k - 1, peer)
            for k, peer in enumerate(along_z, 1)
        ]

    def reduce_along_x(before):
        for each in before:
            each.wait_recv()
        part = weight_parts[torus.z]
        for k in range(nz - 1):
            part = part + z_arrived[k]
        x_sums[torus.x] = part
        return [
            start(x_sums.at[torus.x], x_sums.at[torus.x], x_send, x_recv, k, peer)
            for k, peer in enumerate(along_x)
        ]

    def gather_along_z(before):
        for each in before:
            each.wait_recv()
        part = x_sums[0]
        for k in range(1, nx):
            part = part + x_sums[k]
        z_sums[torus.z] = part * grad_scale
        return [
            start(z_sums.at[torus.z], z_sums.at[torus.z], zz_send, zz_recv, k, peer)
            for k, peer in enumerate(along_z)
        ]

    def gather_along_col(before):
        for each in before:
            each.wait_recv()
        weight_sums[col] = z_sums[...].reshape(weight_sums.shape[1:]).astype(weight_sums.dtype)
        return [
            start(weight_sums.at[col], weight_sums.at[col], cc_send, cc_recv, k, peer)
            for k, peer in enumerate(along_col)
        ]

    def carry(index, source):
        axis, sign, _, count, _ = transfers[index]
        return start(
            source,
            arrived.at[index, pl.ds(0, count)],
            send_sem,
            recv_sem,
            index,
            torus.neighbour(axis, -sign),
        )

    def sum_of(node, carried):
        _, first, full = split[node[0]]
        value = partial[torus.row(node[1], node[2]), first : first + full].astype(jnp.float32)
        for index in reversed(carried):
            lead, count = transfers[index][2:4]
            sent[index].wait_recv()
            came = arrived[index, :count].astype(jnp.float32)
            if count < full:
                filler = jnp.zeros((full - count, came.shape[1]), jnp.float32)
                came = jnp.concatenate([came, filler] if lead == first else [filler, came], axis=0)
            value = value + came
        return value

    sent = {}
    pending = []
    steps = [reduce_along_z, multiply_self, reduce_along_x, gather_along_z, gather_along_col]
    n_parts = len(split)
    inner = sum(1 for _, brought, carried in order if brought and carried)
    stages = {inner * at // 100: step for at, step in zip(STAGES, steps)}
    seen = 0
    for node, brought, carried in reversed(order[2 * n_parts :]):
        begin = split[node[0]][1]
        if carried:
            if seen in stages:
                pending = stages[seen](pending)
            seen += 1
            full = split[node[0]][2]
            home = next(index for index in carried if transfers[index][3] == full)
            if len(carried) == 1:
                sent[home].wait_recv()
                arrived[home, :full] += partial[torus.row(node[1], node[2]), begin : begin + full]
            else:
                arrived[home, :full] = sum_of(node, carried).astype(arrived.dtype)
        for index in reversed(brought):
            first, count = transfers[index][2:4]
            if carried:
                source = arrived.at[home, pl.ds(first - begin, count)]
            else:
                source = partial.at[torus.row(node[1], node[2]), pl.ds(first, count)]
            sent[index] = carry(index, source)

    sums = []
    for (node, _, first_carried), (_, _, carried) in zip(order[:n_parts], order[n_parts:]):
        sums.append((split[node[0]][1], sum_of(node, first_carried + carried)))
    neighbour_sum = jnp.concatenate([part for _, part in sorted(sums, key=lambda pair: pair[0])], axis=0)
    moved_in[...] = (self_grad[...] + neighbour_sum).astype(moved_in.dtype)
    for each in pending:
        each.wait_recv()


def layer_kernel(
    transfers, order, split, nx, nz, n_col, grad_scale,
    slots, row_chain, column_chain,
    features_in, grad_out_in, degrees_in, w_self_in, w_neigh_in, bias_in, masks_in,
    layer_out, moved_in, weight_sums,
    features, grad_out, degrees, w_self, w_neigh, bias, masks,
    own, panel, sums, partial, grad_preact, upward_rows, weight_parts, spread,
    own_part, scale, from_sibling, joined, y_arrived, own_sum, upward, mean_rows, parts, parts_arrived,
    arrived, self_grad, z_arrived, x_sums, z_sums,
    load_sem, own_sem, ring_send, ring_recv, back_send, back_recv, keep_sem, *sems,
):
    torus = Torus(nx, nz)
    col = lax.axis_index("col")
    start = Sender()
    loads = [
        pltpu.make_async_copy(source, target, load_sem.at[k])
        for k, (source, target) in enumerate(
            (
                (features_in, features),
                (w_self_in, w_self),
                (degrees_in, degrees),
                (bias_in, bias),
                (grad_out_in, grad_out),
                (w_neigh_in, w_neigh),
                (masks_in, masks),
            )
        )
    ]
    for each in loads:
        each.start()
    barrier = pltpu.get_barrier_semaphore()
    around = [torus.neighbour(axis, sign) for axis in "xz" for sign in (1, -1)]
    around.append({"col": col + 1 - 2 * lax.rem(col, 2)})
    around += [{"col": lax.rem(col + k, n_col)} for k in range(2, n_col, 2)]
    greet(barrier, around)
    loads[0].wait()
    own[...] = jnp.dot(
        row_order(own.shape[0]), features[...], preferred_element_type=jnp.float32
    ).astype(own.dtype)
    keep = pltpu.make_async_copy(own, panel.at[torus.row(0, 0)], own_sem)
    keep.start()
    pl.semaphore_wait(barrier, len(around))

    roots = 2 * len(split)
    sent = gather_phase(start, torus, transfers, order[:roots], own, panel, ring_send, ring_recv, {})
    size, width = features.shape
    for each in loads[1:]:
        each.wait()
    scale[...] = jnp.broadcast_to(degrees[...].astype(jnp.float32), (width, size)).T
    own_part[...] = bias[...] + jnp.dot(
        features[...], w_self[...], preferred_element_type=jnp.float32
    )
    sums[0] = jnp.zeros(sums.shape[1:], sums.dtype)
    gather_phase(start, torus, transfers, order[roots:], own, panel, ring_send, ring_recv, sent)
    keep.wait()

    n_tiles, block_rows = masks.shape[0], partial.shape[0]
    in_row = size // TILE

    def aggregate(slot, bits):
        block = lax.div(slot, block_rows)
        source = panel[lax.div(block, in_row), pl.ds(lax.rem(block, in_row) * TILE, TILE)]
        return lax.dot_general(bits, source, (((0,), (0,)), ((), ())), preferred_element_type=jnp.float32)

    chain_tiles(slots, row_chain, masks, sums, aggregate)
    for k in range(block_rows):
        partial[k] = sums[row_chain[n_tiles + k]].astype(partial.dtype)

    middle_phase(
        start, col, partial, features, grad_out, w_neigh, layer_out, grad_preact, upward_rows, weight_parts,
        own_part, scale, from_sibling, joined, y_arrived, own_sum, upward, mean_rows, parts, parts_arrived,
        keep_sem, *sems[:10],
    )

    def spread_tile(slot, bits):
        return jnp.dot(bits, upward_rows[lax.rem(slot, block_rows)], preferred_element_type=jnp.float32)

    chain_tiles(slots, column_chain, masks, sums, spread_tile)
    for k in range(spread.shape[0] * in_row):
        here = slice(k % in_row * TILE, (k % in_row + 1) * TILE)
        spread[k // in_row, here] = sums[column_chain[n_tiles + k]].astype(spread.dtype)

    scatter_phase(
        start, torus, col, transfers, order, split, n_col, grad_scale, spread, weight_parts, grad_preact, w_self,
        moved_in, weight_sums, arrived, self_grad, z_arrived, x_sums, z_sums,
        back_send, back_recv, *sems[10:],
    )
    for each in start.started:
        each.wait_send()


def finish_kernel(layer_in, moved_in, weight_sums, layer_out, grad_in, grad_self, grad_neigh):
    layer_out[...] = layer_in[...]
    grad_in[...] = lax.dot_general(
        row_order(moved_in.shape[0]), moved_in[...], (((0,), (0,)), ((), ())), preferred_element_type=jnp.float32
    ).astype(grad_in.dtype)
    rows = weight_sums.shape[1] // 2
    for c in range(weight_sums.shape[0]):
        grad_self[c * rows : (c + 1) * rows] = weight_sums[c, :rows].astype(grad_self.dtype)
        grad_neigh[c * rows : (c + 1) * rows] = weight_sums[c, rows:].astype(grad_neigh.dtype)


def array(dtype, *shape):
    return jax.ShapeDtypeStruct(shape, dtype)


def chains(keys, live, blocks):
    tiles = jnp.arange(keys.shape[0], dtype=jnp.int32)
    asked = jnp.concatenate([keys, jnp.arange(blocks, dtype=jnp.int32)])
    until = jnp.concatenate([tiles, jnp.full((blocks,), keys.shape[0], jnp.int32)])
    found = (tiles[None, :] < jnp.minimum(until[:, None], live)) & (keys[None, :] == asked[:, None])
    return jnp.max(jnp.where(found, tiles[None, :] + 1, 0), axis=1)


def shards(features, grad_out, degrees, w_self, w_neigh, bias, tile_slots, tile_count, tile_masks):
    size, width = features.shape
    n_row, n_col = lax.axis_size("row"), lax.axis_size("col")
    nx, nz = 4, n_row // 4
    ny, halves = n_col // 2, size // TILE
    split = [("xz", 0, 48), ("xz", 48, 48), ("zx", 96, 80), ("zx", 176, 80)]
    transfers, order = torus_plan(nx, nz, split)
    copies = len(transfers)
    bf16, f32, i32 = jnp.bfloat16, jnp.float32, jnp.int32
    dma = pltpu.SemaphoreType.DMA
    slots, live, masks = tile_slots[0, 0], tile_count[0, 0], tile_masks[0, 0]
    n_tiles = masks.shape[0]
    block_rows = n_col * halves
    block_columns = n_row * halves
    row_chain = chains(slots % block_rows, live, block_rows)
    column_chain = chains(slots // block_rows, live, block_columns)
    grad_scale = 1.0 / math.sqrt(size * n_row * n_col)
    grad_rows = 2 * width // n_col
    z_rows = grad_rows // nz
    others = n_col - 1
    y_copies = (ny - 1) * halves

    layer_in, moved_in, weight_sums = pl.pallas_call(
        functools.partial(layer_kernel, transfers, order, split, nx, nz, n_col, grad_scale),
        name="layer",
        out_shape=(
            array(bf16, size, width),
            array(bf16, size, width),
            array(bf16, n_col, grad_rows, width),
        ),
        in_specs=[SMEM] * 3 + [ANY] * 7,
        out_specs=(VMEM, VMEM, VMEM),
        scratch_shapes=[
            pltpu.VMEM((size, width), bf16),
            pltpu.VMEM((size, width), bf16),
            pltpu.VMEM((1, size), i32),
            pltpu.VMEM((width, width), bf16),
            pltpu.VMEM((width, width), bf16),
            pltpu.VMEM((1, width), f32),
            pltpu.VMEM(masks.shape, i32),
            pltpu.VMEM((size, width), bf16),
            pltpu.VMEM((n_row, size, width), bf16),
            pltpu.VMEM((n_tiles + 1, TILE, width), f32),
            pltpu.VMEM((block_rows, TILE, width), bf16),
            pltpu.VMEM((size, width), bf16),
            pltpu.VMEM((block_rows, TILE, width), bf16),
            pltpu.VMEM((nz, z_rows, width), f32),
            pltpu.VMEM((n_row, size, width), bf16),
            pltpu.VMEM((size, width), f32),
            pltpu.VMEM((size, width), f32),
            pltpu.VMEM((ny, halves, TILE, width), bf16),
            pltpu.VMEM((ny - 1, halves, TILE, width), bf16),
            pltpu.VMEM((ny - 1, halves, TILE, width), bf16),
            pltpu.VMEM((halves, TILE, width), f32),
            pltpu.VMEM((halves, TILE, width), bf16),
            pltpu.VMEM((size, width), bf16),
            pltpu.VMEM((n_col, grad_rows, width), bf16),
            pltpu.VMEM((others, grad_rows, width), bf16),
            pltpu.VMEM((copies, max(part[2] for part in split), width), bf16),
            pltpu.VMEM((size, width), f32),
            pltpu.VMEM((nz - 1, z_rows, width), f32),
            pltpu.VMEM((nx, z_rows, width), f32),
            pltpu.VMEM((nz, z_rows, width), f32),
            dma((7,)),
            dma,
        ]
        + [dma((copies,))] * 4
        + [dma((halves,))]
        + [dma((ny * halves,))] * 2
        + [dma((y_copies,))] * 4
        + [dma((ny * halves,))] * 2
        + [dma((others,))] * 2
        + [dma((nz - 1,))] * 2
        + [dma((nx - 1,))] * 2
        + [dma((nz - 1,))] * 2
        + [dma((others,))] * 2,
        compiler_params=pltpu.CompilerParams(
            collective_id=0, has_side_effects=True, vmem_limit_bytes=58 << 20
        ),
    )(
        slots,
        row_chain,
        column_chain,
        features,
        grad_out,
        degrees[None, :],
        w_self,
        w_neigh,
        bias[None, :],
        masks,
    )

    return pl.pallas_call(
        finish_kernel,
        name="finish",
        out_shape=(
            array(bf16, size, width),
            array(bf16, size, width),
            array(f32, width, width),
            array(f32, width, width),
        ),
        in_specs=[VMEM] * 3,
        out_specs=(VMEM,) * 4,
        compiler_params=pltpu.CompilerParams(vmem_limit_bytes=8 << 20),
    )(layer_in, moved_in, weight_sums)


def solution(mesh):
    placed = (
        P(("row", "col"), None),
        P(("row", "col"), None),
        P(("row", "col")),
        P(),
        P(),
        P(),
        P("row", "col", None),
        P("row", "col"),
        P("row", "col", None, None, None),
    )
    return jax.shard_map(
        shards,
        mesh=mesh,
        in_specs=placed,
        out_specs=(P(("row", "col"), None), P(("row", "col"), None), P(), P()),
        check_vma=False,
    )
```

```python
import functools
import heapq
import math

import jax
import jax.numpy as jnp
from jax import lax
from jax.experimental import pallas as pl
from jax.experimental.pallas import tpu as pltpu
from jax.sharding import PartitionSpec as P

MESH = pl.DeviceIdType.MESH
SMEM = pl.BlockSpec(memory_space=pltpu.SMEM)
VMEM = pl.BlockSpec(memory_space=pltpu.VMEM)
ANY = pl.BlockSpec(memory_space=pl.ANY)
TILE = 128
UNROLL = 16
STAGES = (0, 2, 18, 38, 58)


def torus_plan(nx, nz, split, latency=4.0, rate=0.0085):
    size = {"x": nx, "z": nz}
    transfers, order = [], []
    free, heap = {}, []

    def wrap(d, n):
        d %= n
        return d - n if d > n // 2 else d

    def send(now, node, axis, sign, first, count):
        offset = {"x": node[1], "z": node[2]}
        offset[axis] = wrap(offset[axis] - sign, size[axis])
        index = len(transfers)
        transfers.append((axis, sign, first, count, (node[0], offset["x"], offset["z"])))
        start = max(now, free.get((axis, sign), 0.0))
        free[axis, sign] = start + count * rate
        heapq.heappush(heap, (free[axis, sign] + latency, index))
        entries[node][1].append(index)

    def forward(now, node, phases="pq"):
        part = node[0]
        (p, q), begin, full = split[part]
        offset = {"x": node[1], "z": node[2]}
        dp, dq = offset[p], offset[q]
        half_p, half_q = size[p] // 2, size[q] // 2
        lower = (full // 2 + 15) // 16 * 16
        for sign in (1, -1) if "p" in phases else ():
            if dq == 0 and (dp == 0 or -dp * sign > 0) and dp != half_p:
                if abs(dp) + 1 < half_p:
                    send(now, node, p, sign, begin, full)
                elif sign == 1:
                    send(now, node, p, sign, begin, lower)
                else:
                    send(now, node, p, sign, begin + lower, full - lower)
        for sign in (1, -1) if "q" in phases else ():
            if (dq == 0 or -dq * sign > 0) and dq != half_q:
                if abs(dq) + 1 < half_q or (0 <= dp < half_p) == (sign == 1):
                    send(now, node, q, sign, begin, full)

    got = {}
    entries = {(part, 0, 0): ([], []) for part in range(len(split))}
    roots = []
    for phases in "pq":
        for part in range(len(split)):
            forward(0.0, (part, 0, 0), phases)
            roots.append(((part, 0, 0), [], entries[part, 0, 0][1]))
            entries[part, 0, 0] = ([], [])
    while heap:
        now, index = heapq.heappop(heap)
        count, node = transfers[index][3:]
        entries.setdefault(node, ([], []))[0].append(index)
        got[node] = got.get(node, 0) + count
        if got[node] == split[node[0]][2]:
            order.append(node)
            forward(now, node)
    return transfers, roots + [(node, *entries[node]) for node in order]


class Torus:
    def __init__(self, nx, nz):
        self.nx, self.nz = nx, nz
        row = lax.axis_index("row")
        self.x, self.z = lax.rem(row, nx), lax.div(row, nx)

    def row(self, dx, dz):
        x = lax.rem(self.x + (dx + self.nx), self.nx)
        z = lax.rem(self.z + (dz + self.nz), self.nz)
        return z * self.nx + x

    def neighbour(self, axis, sign):
        return {"row": self.row(sign, 0) if axis == "x" else self.row(0, sign)}


def greet(barrier, peers):
    for peer in peers:
        pl.semaphore_signal(barrier, inc=1, device_id=peer, device_id_type=MESH)


def row_order(size):
    place = lax.broadcasted_iota(jnp.int32, (size, size), 0)
    node = lax.broadcasted_iota(jnp.int32, (size, size), 1)
    within = place & (TILE - 1)
    source = (place - within) + ((within & 15) << 3) + (within >> 4)
    return jnp.where(source == node, 1.0, 0.0).astype(jnp.bfloat16)


class Sender:
    def __init__(self):
        self.started = []

    def __call__(self, source, target, sends, recvs, k, peer):
        copy = pltpu.make_async_remote_copy(
            src_ref=source,
            dst_ref=target,
            send_sem=sends.at[k],
            recv_sem=recvs.at[k],
            device_id=peer,
            device_id_type=MESH,
        )
        copy.start()
        self.started.append(copy)
        return copy


def gather_phase(start, torus, transfers, order, own, panel, send_sem, recv_sem, sent):
    for node, brought, carried in order:
        for index in brought:
            sent[index].wait_recv()
        origin = torus.row(node[1], node[2])
        for index in carried:
            axis, sign, first, count, _ = transfers[index]
            rows = pl.ds(first, count)
            sent[index] = start(
                panel.at[origin, rows] if brought else own.at[rows],
                panel.at[origin, rows],
                send_sem,
                recv_sem,
                index,
                torus.neighbour(axis, sign),
            )
    return sent


def unpack(words):
    return jnp.concatenate(
        [((words >> bit) & 1).astype(jnp.float32).astype(jnp.bfloat16) for bit in range(8)], axis=0
    )


def write_chains(slots_row, live, block_rows, n_tiles, chains):
    lanes = chains.shape[1]
    asked_slot = jnp.concatenate(
        [slots_row[...], jnp.zeros((1, lanes - n_tiles), jnp.int32)], axis=1
    )
    place = lax.broadcasted_iota(jnp.int32, (1, lanes), 1)
    tile = lax.broadcasted_iota(jnp.int32, (lanes, lanes), 0)
    slot = jnp.broadcast_to(asked_slot, (lanes, lanes)).T
    until = jnp.minimum(jnp.where(place < n_tiles, place, n_tiles), live)
    shift = block_rows.bit_length() - 1
    for k in range(2):
        key = slot & (block_rows - 1) if k == 0 else slot >> shift
        asked = asked_slot & (block_rows - 1) if k == 0 else asked_slot >> shift
        asked = jnp.where(place < n_tiles, asked, place - n_tiles)
        found = jnp.where((tile < until) & (key == asked), tile + 1, 0)
        chains[k : k + 1] = jnp.max(found, axis=0, keepdims=True)


def chain_tiles(slots, before, which, masks, sums, product):
    def group(index, _):
        for u in range(UNROLL):
            tile = index * UNROLL + u
            sums[tile + 1] = sums[before[which, tile]] + product(slots[tile], unpack(masks[tile]))
        return 0

    lax.fori_loop(0, masks.shape[0] // UNROLL, group, 0)


def middle_phase(
    start, col, partial, features, grad_out, w_neigh, layer_out, grad_preact, upward_rows, weight_parts,
    own_part, scale, from_sibling, joined, arrived, own_sum, upward, mean_rows, parts, parts_arrived,
    keep_sem, sibling_send, sibling_recv, y_send, y_recv, up_send, up_recv, pass_send, pass_recv, w_send, w_recv,
):
    y, core = lax.div(col, 2), lax.rem(col, 2)
    ny, halves, rows = from_sibling.shape[:3]
    n_col = 2 * ny
    width = features.shape[1]
    place = [lax.rem(y + k, ny) for k in range(ny)]
    far_first = sorted(range(1, ny), key=lambda k: -min(k, ny - k))
    sibling = {"col": 2 * y + 1 - core}
    along_y = [{"col": 2 * place[k] + core} for k in range(ny)]
    along_col = [{"col": lax.rem(col + k, n_col)} for k in range(1, n_col)]
    pieces = [(half, k) for half in range(halves) for k in (*far_first, 0)]
    shared = {}
    for half, k in pieces:
        shared[half, k] = start(
            partial.at[4 * place[k] + 2 * (1 - core) + half], from_sibling.at[k, half],
            sibling_send, sibling_recv, half * ny + k, sibling,
        )
    exchanged = {}
    for half, k in pieces:
        shared[half, k].wait_recv()
        both = partial[4 * place[k] + 2 * core + half].astype(jnp.float32)
        both = both + from_sibling[k, half].astype(jnp.float32)
        if k == 0:
            own_sum[half] = both
        else:
            joined[k - 1, half] = both.astype(joined.dtype)
            exchanged[half, k] = start(
                joined.at[k - 1, half], arrived.at[k - 1, half],
                y_send, y_recv, half * (ny - 1) + k - 1, along_y[k],
            )
    gathered, passed, kept = {}, [], []
    for half in range(halves):
        summed = own_sum[half]
        for k in far_first:
            exchanged[half, k].wait_recv()
            summed = summed + arrived[k - 1, half].astype(jnp.float32)
        here = slice(half * rows, (half + 1) * rows)
        mean = (summed / scale[here]).astype(mean_rows.dtype)
        preact = own_part[here] + jnp.dot(mean, w_neigh[...], preferred_element_type=jnp.float32)
        sigmoid_values = jax.nn.sigmoid(preact)
        gradient = (
            grad_out[here].astype(jnp.float32) * sigmoid_values * (1.0 + preact * (1.0 - sigmoid_values))
        ).astype(grad_preact.dtype)
        sent_up = lax.dot_general(
            gradient, w_neigh[...], (((1,), (1,)), ((), ())), preferred_element_type=jnp.float32
        )
        upward[half] = (sent_up / scale[here]).astype(upward.dtype)
        target = upward_rows.at[2 * col + half]
        for k in far_first:
            gathered[half, k] = start(
                upward.at[half], target, up_send, up_recv, half * (ny - 1) + k - 1, along_y[k]
            )
        passed.append(start(upward.at[half], target, pass_send, pass_recv, half * ny, sibling))
        kept.append(pltpu.make_async_copy(upward.at[half], target, keep_sem.at[half]))
        kept[-1].start()
        layer_out[here] = (preact * sigmoid_values).astype(layer_out.dtype)
        mean_rows[here] = mean
        grad_preact[here] = gradient
    part_rows = width // n_col
    for which, source in enumerate((features, mean_rows)):
        product = lax.dot_general(
            source[...], grad_preact[...], (((0,), (0,)), ((), ())), preferred_element_type=jnp.float32
        ).astype(parts.dtype)
        for c in range(n_col):
            parts[c, which * part_rows : (which + 1) * part_rows] = product[
                c * part_rows : (c + 1) * part_rows
            ]
    reduced = [
        start(parts.at[lax.rem(col + k, n_col)], parts_arrived.at[k - 1], w_send, w_recv, k - 1, peer)
        for k, peer in enumerate(along_col, 1)
    ]
    for half in range(halves):
        for k in reversed(far_first):
            gathered[half, k].wait_recv()
            held = upward_rows.at[4 * lax.rem(y + ny - k, ny) + 2 * core + half]
            passed.append(start(held, held, pass_send, pass_recv, half * ny + k, sibling))
    total = parts[col].astype(jnp.float32)
    for k, each in enumerate(reduced):
        each.wait_recv()
        total = total + parts_arrived[k].astype(jnp.float32)
    weight_parts[...] = total.reshape(weight_parts.shape)
    for each in passed:
        each.wait_recv()
    for each in kept:
        each.wait()


def scatter_phase(
    start, torus, col, transfers, order, split, n_col, grad_scale, partial, round_owner, weight_parts, grad_preact, w_self,
    moved_in, weight_sums, arrived, self_grad, z_arrived, x_sums, z_sums,
    send_sem, recv_sem, z_send, z_recv, x_send, x_recv, zz_send, zz_recv, cc_send, cc_recv,
):
    nx, nz = torus.nx, torus.nz
    along_col = [{"col": lax.rem(col + k, n_col)} for k in range(1, n_col)]
    along_z = [{"row": torus.row(0, k)} for k in range(1, nz)]
    along_x = [{"row": torus.row(k, 0)} for k in range(1, nx)]

    def multiply_self(before):
        moved = jnp.dot(
            row_order(grad_preact.shape[0]), grad_preact[...], preferred_element_type=jnp.float32
        ).astype(jnp.bfloat16)
        self_grad[...] = lax.dot_general(
            moved, w_self[...], (((1,), (1,)), ((), ())), preferred_element_type=jnp.float32
        )
        return before

    def reduce_along_z(_):
        return [
            start(weight_parts.at[lax.rem(torus.z + k, nz)], z_arrived.at[k - 1], z_send, z_recv, k - 1, peer)
            for k, peer in enumerate(along_z, 1)
        ]

    def reduce_along_x(before):
        for each in before:
            each.wait_recv()
        part = weight_parts[torus.z]
        for k in range(nz - 1):
            part = part + z_arrived[k]
        x_sums[torus.x] = part
        return [
            start(x_sums.at[torus.x], x_sums.at[torus.x], x_send, x_recv, k, peer)
            for k, peer in enumerate(along_x)
        ]

    def gather_along_z(before):
        for each in before:
            each.wait_recv()
        part = x_sums[0]
        for k in range(1, nx):
            part = part + x_sums[k]
        z_sums[torus.z] = part * grad_scale
        return [
            start(z_sums.at[torus.z], z_sums.at[torus.z], zz_send, zz_recv, k, peer)
            for k, peer in enumerate(along_z)
        ]

    def gather_along_col(before):
        for each in before:
            each.wait_recv()
        weight_sums[col] = z_sums[...].reshape(weight_sums.shape[1:]).astype(weight_sums.dtype)
        return [
            start(weight_sums.at[col], weight_sums.at[col], cc_send, cc_recv, k, peer)
            for k, peer in enumerate(along_col)
        ]

    def carry(index, source):
        axis, sign, _, count, _ = transfers[index]
        return start(
            source,
            arrived.at[index, pl.ds(0, count)],
            send_sem,
            recv_sem,
            index,
            torus.neighbour(axis, -sign),
        )

    def sum_of(node, carried):
        _, first, full = split[node[0]]
        value = partial[torus.row(node[1], node[2]), first : first + full].astype(jnp.float32)
        for index in reversed(carried):
            lead, count = transfers[index][2:4]
            sent[index].wait_recv()
            came = arrived[index, :count].astype(jnp.float32)
            if count < full:
                filler = jnp.zeros((full - count, came.shape[1]), jnp.float32)
                came = jnp.concatenate([came, filler] if lead == first else [filler, came], axis=0)
            value = value + came
        return value

    sent = {}
    pending = []
    steps = [reduce_along_z, multiply_self, reduce_along_x, gather_along_z, gather_along_col]
    n_parts = len(split)
    inner = sum(1 for _, brought, carried in order if brought and carried)
    stages = {inner * at // 100: step for at, step in zip(STAGES, steps)}
    seen = 0
    rounded = set()
    for node, brought, carried in reversed(order[2 * n_parts :]):
        begin = split[node[0]][1]
        if node[1:] not in rounded:
            rounded.add(node[1:])
            round_owner(torus.row(*node[1:]))
        if carried:
            if seen in stages:
                pending = stages[seen](pending)
            seen += 1
            full = split[node[0]][2]
            home = next(index for index in carried if transfers[index][3] == full)
            if len(carried) == 1:
                sent[home].wait_recv()
                arrived[home, :full] += partial[torus.row(node[1], node[2]), begin : begin + full]
            else:
                arrived[home, :full] = sum_of(node, carried).astype(arrived.dtype)
        for index in reversed(brought):
            first, count = transfers[index][2:4]
            if carried:
                source = arrived.at[home, pl.ds(first - begin, count)]
            else:
                source = partial.at[torus.row(node[1], node[2]), pl.ds(first, count)]
            sent[index] = carry(index, source)

    round_owner(torus.row(0, 0))
    sums = []
    for (node, _, first_carried), (_, _, carried) in zip(order[:n_parts], order[n_parts:]):
        sums.append((split[node[0]][1], sum_of(node, first_carried + carried)))
    neighbour_sum = jnp.concatenate([part for _, part in sorted(sums, key=lambda pair: pair[0])], axis=0)
    moved_in[...] = (self_grad[...] + neighbour_sum).astype(moved_in.dtype)
    for each in pending:
        each.wait_recv()


def layer_kernel(
    transfers, order, split, nx, nz, n_col, grad_scale,
    slots, live, slots_in,
    features_in, grad_out_in, degrees_in, w_self_in, w_neigh_in, bias_in, masks_in,
    layer_out, moved_in, weight_sums,
    slots_row, features, grad_out, degrees, w_self, w_neigh, bias, masks,
    own, panel, sums, partial, grad_preact, upward_rows, weight_parts, spread,
    own_part, scale, from_sibling, joined, y_arrived, own_sum, upward, mean_rows, parts, parts_arrived,
    arrived, self_grad, z_arrived, x_sums, z_sums,
    chains, before, load_sem, own_sem, chain_sem, ring_send, ring_recv, back_send, back_recv, keep_sem, *sems,
):
    torus = Torus(nx, nz)
    col = lax.axis_index("col")
    start = Sender()
    loads = [
        pltpu.make_async_copy(source, target, load_sem.at[k])
        for k, (source, target) in enumerate(
            (
                (features_in, features),
                (slots_in, slots_row),
                (w_self_in, w_self),
                (degrees_in, degrees),
                (bias_in, bias),
                (grad_out_in, grad_out),
                (w_neigh_in, w_neigh),
                (masks_in, masks),
            )
        )
    ]
    for each in loads:
        each.start()
    barrier = pltpu.get_barrier_semaphore()
    around = [torus.neighbour(axis, sign) for axis in "xz" for sign in (1, -1)]
    around.append({"col": col + 1 - 2 * lax.rem(col, 2)})
    around += [{"col": lax.rem(col + k, n_col)} for k in range(2, n_col, 2)]
    greet(barrier, around)
    loads[0].wait()
    own[...] = jnp.dot(
        row_order(own.shape[0]), features[...], preferred_element_type=jnp.float32
    ).astype(own.dtype)
    keep = pltpu.make_async_copy(own, panel.at[torus.row(0, 0)], own_sem)
    keep.start()
    pl.semaphore_wait(barrier, len(around))

    roots = 2 * len(split)
    sent = gather_phase(start, torus, transfers, order[:roots], own, panel, ring_send, ring_recv, {})
    n_tiles, block_rows = masks.shape[0], partial.shape[0]
    loads[1].wait()
    write_chains(slots_row, live[0], block_rows, n_tiles, chains)
    tables = pltpu.make_async_copy(chains, before, chain_sem)
    tables.start()
    size, width = features.shape
    for each in loads[2:]:
        each.wait()
    scale[...] = jnp.broadcast_to(degrees[...].astype(jnp.float32), (width, size)).T
    own_part[...] = bias[...] + jnp.dot(
        features[...], w_self[...], preferred_element_type=jnp.float32
    )
    sums[0] = jnp.zeros(sums.shape[1:], sums.dtype)
    gather_phase(start, torus, transfers, order[roots:], own, panel, ring_send, ring_recv, sent)
    keep.wait()
    tables.wait()

    in_row = size // TILE

    def aggregate(slot, bits):
        block = lax.div(slot, block_rows)
        source = panel[lax.div(block, in_row), pl.ds(lax.rem(block, in_row) * TILE, TILE)]
        return lax.dot_general(bits, source, (((0,), (0,)), ((), ())), preferred_element_type=jnp.float32)

    chain_tiles(slots, before, 0, masks, sums, aggregate)
    for k in range(block_rows):
        partial[k] = sums[before[0, n_tiles + k]].astype(partial.dtype)

    middle_phase(
        start, col, partial, features, grad_out, w_neigh, layer_out, grad_preact, upward_rows, weight_parts,
        own_part, scale, from_sibling, joined, y_arrived, own_sum, upward, mean_rows, parts, parts_arrived,
        keep_sem, *sems[:10],
    )

    def spread_tile(slot, bits):
        return jnp.dot(bits, upward_rows[lax.rem(slot, block_rows)], preferred_element_type=jnp.float32)

    chain_tiles(slots, before, 1, masks, sums, spread_tile)

    def round_owner(owner):
        for k in range(in_row):
            last = before[1, n_tiles + owner * in_row + k]
            spread[owner, k * TILE : (k + 1) * TILE] = sums[last].astype(spread.dtype)

    scatter_phase(
        start, torus, col, transfers, order, split, n_col, grad_scale, spread, round_owner, weight_parts, grad_preact, w_self,
        moved_in, weight_sums, arrived, self_grad, z_arrived, x_sums, z_sums,
        back_send, back_recv, *sems[10:],
    )
    for each in start.started:
        each.wait_send()


def finish_kernel(layer_in, moved_in, weight_sums, layer_out, grad_in, grad_self, grad_neigh):
    layer_out[...] = layer_in[...]
    grad_in[...] = lax.dot_general(
        row_order(moved_in.shape[0]), moved_in[...], (((0,), (0,)), ((), ())), preferred_element_type=jnp.float32
    ).astype(grad_in.dtype)
    rows = weight_sums.shape[1] // 2
    for c in range(weight_sums.shape[0]):
        grad_self[c * rows : (c + 1) * rows] = weight_sums[c, :rows].astype(grad_self.dtype)
        grad_neigh[c * rows : (c + 1) * rows] = weight_sums[c, rows:].astype(grad_neigh.dtype)


def array(dtype, *shape):
    return jax.ShapeDtypeStruct(shape, dtype)


def shards(features, grad_out, degrees, w_self, w_neigh, bias, tile_slots, tile_count, tile_masks):
    size, width = features.shape
    n_row, n_col = lax.axis_size("row"), lax.axis_size("col")
    nx, nz = 4, n_row // 4
    ny, halves = n_col // 2, size // TILE
    split = [("xz", 0, 48), ("xz", 48, 48), ("zx", 96, 80), ("zx", 176, 80)]
    transfers, order = torus_plan(nx, nz, split)
    copies = len(transfers)
    bf16, f32, i32 = jnp.bfloat16, jnp.float32, jnp.int32
    dma = pltpu.SemaphoreType.DMA
    slots, live, masks = tile_slots[0, 0], tile_count[0], tile_masks[0, 0]
    n_tiles = masks.shape[0]
    block_rows = n_col * halves
    block_columns = n_row * halves
    places = -(-(n_tiles + max(block_rows, block_columns)) // TILE) * TILE
    grad_scale = 1.0 / math.sqrt(size * n_row * n_col)
    grad_rows = 2 * width // n_col
    z_rows = grad_rows // nz
    others = n_col - 1
    y_copies = (ny - 1) * halves

    layer_in, moved_in, weight_sums = pl.pallas_call(
        functools.partial(layer_kernel, transfers, order, split, nx, nz, n_col, grad_scale),
        name="layer",
        out_shape=(
            array(bf16, size, width),
            array(bf16, size, width),
            array(bf16, n_col, grad_rows, width),
        ),
        in_specs=[SMEM, SMEM] + [ANY] * 8,
        out_specs=(VMEM, VMEM, VMEM),
        scratch_shapes=[
            pltpu.VMEM((1, n_tiles), i32),
            pltpu.VMEM((size, width), bf16),
            pltpu.VMEM((size, width), bf16),
            pltpu.VMEM((1, size), i32),
            pltpu.VMEM((width, width), bf16),
            pltpu.VMEM((width, width), bf16),
            pltpu.VMEM((1, width), f32),
            pltpu.VMEM(masks.shape, i32),
            pltpu.VMEM((size, width), bf16),
            pltpu.VMEM((n_row, size, width), bf16),
            pltpu.VMEM((n_tiles + 1, TILE, width), f32),
            pltpu.VMEM((block_rows, TILE, width), bf16),
            pltpu.VMEM((size, width), bf16),
            pltpu.VMEM((block_rows, TILE, width), bf16),
            pltpu.VMEM((nz, z_rows, width), f32),
            pltpu.VMEM((n_row, size, width), bf16),
            pltpu.VMEM((size, width), f32),
            pltpu.VMEM((size, width), f32),
            pltpu.VMEM((ny, halves, TILE, width), bf16),
            pltpu.VMEM((ny - 1, halves, TILE, width), bf16),
            pltpu.VMEM((ny - 1, halves, TILE, width), bf16),
            pltpu.VMEM((halves, TILE, width), f32),
            pltpu.VMEM((halves, TILE, width), bf16),
            pltpu.VMEM((size, width), bf16),
            pltpu.VMEM((n_col, grad_rows, width), bf16),
            pltpu.VMEM((others, grad_rows, width), bf16),
            pltpu.VMEM((copies, max(part[2] for part in split), width), bf16),
            pltpu.VMEM((size, width), f32),
            pltpu.VMEM((nz - 1, z_rows, width), f32),
            pltpu.VMEM((nx, z_rows, width), f32),
            pltpu.VMEM((nz, z_rows, width), f32),
            pltpu.VMEM((2, places), i32),
            pltpu.SMEM((2, places), i32),
            dma((8,)),
            dma,
            dma,
        ]
        + [dma((copies,))] * 4
        + [dma((halves,))]
        + [dma((ny * halves,))] * 2
        + [dma((y_copies,))] * 4
        + [dma((ny * halves,))] * 2
        + [dma((others,))] * 2
        + [dma((nz - 1,))] * 2
        + [dma((nx - 1,))] * 2
        + [dma((nz - 1,))] * 2
        + [dma((others,))] * 2,
        compiler_params=pltpu.CompilerParams(
            collective_id=0, has_side_effects=True, vmem_limit_bytes=58 << 20
        ),
    )(
        slots,
        live,
        slots[None, :],
        features,
        grad_out,
        degrees[None, :],
        w_self,
        w_neigh,
        bias[None, :],
        masks,
    )

    return pl.pallas_call(
        finish_kernel,
        name="finish",
        out_shape=(
            array(bf16, size, width),
            array(bf16, size, width),
            array(f32, width, width),
            array(f32, width, width),
        ),
        in_specs=[VMEM] * 3,
        out_specs=(VMEM,) * 4,
        compiler_params=pltpu.CompilerParams(vmem_limit_bytes=58 << 20),
    )(layer_in, moved_in, weight_sums)


def solution(mesh):
    placed = (
        P(("row", "col"), None),
        P(("row", "col"), None),
        P(("row", "col")),
        P(),
        P(),
        P(),
        P("row", "col", None),
        P("row", "col"),
        P("row", "col", None, None, None),
    )
    return jax.shard_map(
        shards,
        mesh=mesh,
        in_specs=placed,
        out_specs=(P(("row", "col"), None), P(("row", "col"), None), P(), P()),
        check_vma=False,
    )
```

```python
import functools
import heapq
import math

import jax
import jax.numpy as jnp
from jax import lax
from jax.experimental import pallas as pl
from jax.experimental.pallas import tpu as pltpu
from jax.sharding import PartitionSpec as P

MESH = pl.DeviceIdType.MESH
SMEM = pl.BlockSpec(memory_space=pltpu.SMEM)
VMEM = pl.BlockSpec(memory_space=pltpu.VMEM)
ANY = pl.BlockSpec(memory_space=pl.ANY)
TILE = 128
UNROLL = 22
STAGES = (0, 2, 18, 38, 58)


def torus_plan(nx, nz, split, latency=4.0, rate=0.0085):
    size = {"x": nx, "z": nz}
    transfers, order = [], []
    free, heap = {}, []

    def wrap(d, n):
        d %= n
        return d - n if d > n // 2 else d

    def send(now, node, axis, sign, first, count):
        offset = {"x": node[1], "z": node[2]}
        offset[axis] = wrap(offset[axis] - sign, size[axis])
        index = len(transfers)
        transfers.append((axis, sign, first, count, (node[0], offset["x"], offset["z"])))
        start = max(now, free.get((axis, sign), 0.0))
        free[axis, sign] = start + count * rate
        heapq.heappush(heap, (free[axis, sign] + latency, index))
        entries[node][1].append(index)

    def forward(now, node, phases="pq"):
        part = node[0]
        (p, q), begin, full = split[part]
        offset = {"x": node[1], "z": node[2]}
        dp, dq = offset[p], offset[q]
        half_p, half_q = size[p] // 2, size[q] // 2
        lower = (full // 2 + 15) // 16 * 16
        for sign in (1, -1) if "p" in phases else ():
            if dq == 0 and (dp == 0 or -dp * sign > 0) and dp != half_p:
                if abs(dp) + 1 < half_p:
                    send(now, node, p, sign, begin, full)
                elif sign == 1:
                    send(now, node, p, sign, begin, lower)
                else:
                    send(now, node, p, sign, begin + lower, full - lower)
        for sign in (1, -1) if "q" in phases else ():
            if (dq == 0 or -dq * sign > 0) and dq != half_q:
                if abs(dq) + 1 < half_q or (0 <= dp < half_p) == (sign == 1):
                    send(now, node, q, sign, begin, full)

    got = {}
    entries = {(part, 0, 0): ([], []) for part in range(len(split))}
    roots = []
    for phases in "pq":
        for part in range(len(split)):
            forward(0.0, (part, 0, 0), phases)
            roots.append(((part, 0, 0), [], entries[part, 0, 0][1]))
            entries[part, 0, 0] = ([], [])
    while heap:
        now, index = heapq.heappop(heap)
        count, node = transfers[index][3:]
        entries.setdefault(node, ([], []))[0].append(index)
        got[node] = got.get(node, 0) + count
        if got[node] == split[node[0]][2]:
            order.append(node)
            forward(now, node)
    return transfers, roots + [(node, *entries[node]) for node in order]


class Torus:
    def __init__(self, nx, nz):
        self.nx, self.nz = nx, nz
        row = lax.axis_index("row")
        self.x, self.z = lax.rem(row, nx), lax.div(row, nx)

    def row(self, dx, dz):
        x = lax.rem(self.x + (dx + self.nx), self.nx)
        z = lax.rem(self.z + (dz + self.nz), self.nz)
        return z * self.nx + x

    def neighbour(self, axis, sign):
        return {"row": self.row(sign, 0) if axis == "x" else self.row(0, sign)}


def greet(barrier, peers):
    for peer in peers:
        pl.semaphore_signal(barrier, inc=1, device_id=peer, device_id_type=MESH)


def row_order(size):
    place = lax.broadcasted_iota(jnp.int32, (size, size), 0)
    node = lax.broadcasted_iota(jnp.int32, (size, size), 1)
    within = place & (TILE - 1)
    source = (place - within) + ((within & 15) << 3) + (within >> 4)
    return jnp.where(source == node, 1.0, 0.0).astype(jnp.bfloat16)


class Sender:
    def __init__(self):
        self.started = []

    def __call__(self, source, target, sends, recvs, k, peer):
        copy = pltpu.make_async_remote_copy(
            src_ref=source,
            dst_ref=target,
            send_sem=sends.at[k],
            recv_sem=recvs.at[k],
            device_id=peer,
            device_id_type=MESH,
        )
        copy.start()
        self.started.append(copy)
        return copy


def gather_phase(start, torus, transfers, order, own, panel, send_sem, recv_sem, sent):
    for node, brought, carried in order:
        for index in brought:
            sent[index].wait_recv()
        origin = torus.row(node[1], node[2])
        for index in carried:
            axis, sign, first, count, _ = transfers[index]
            rows = pl.ds(first, count)
            sent[index] = start(
                panel.at[origin, rows] if brought else own.at[rows],
                panel.at[origin, rows],
                send_sem,
                recv_sem,
                index,
                torus.neighbour(axis, sign),
            )
    return sent


def unpack(words):
    return jnp.concatenate(
        [((words >> bit) & 1).astype(jnp.float32).astype(jnp.bfloat16) for bit in range(8)], axis=0
    )


def write_chains(slots_row, live, block_rows, n_tiles, chains):
    lanes = chains.shape[1]
    asked_slot = jnp.concatenate(
        [slots_row[...], jnp.zeros((1, lanes - n_tiles), jnp.int32)], axis=1
    )
    place = lax.broadcasted_iota(jnp.int32, (1, lanes), 1)
    tile = lax.broadcasted_iota(jnp.int32, (lanes, lanes), 0)
    slot = jnp.broadcast_to(asked_slot, (lanes, lanes)).T
    until = jnp.minimum(jnp.where(place < n_tiles, place, n_tiles), live)
    shift = block_rows.bit_length() - 1
    for k in range(2):
        key = slot & (block_rows - 1) if k == 0 else slot >> shift
        asked = asked_slot & (block_rows - 1) if k == 0 else asked_slot >> shift
        asked = jnp.where(place < n_tiles, asked, place - n_tiles)
        found = jnp.where((tile < until) & (key == asked), tile + 1, 0)
        chains[k : k + 1] = jnp.max(found, axis=0, keepdims=True)


def chain_tiles(slots, before, which, masks, sums, product):
    def group(index, _):
        for u in range(UNROLL):
            tile = index * UNROLL + u
            sums[tile + 1] = sums[before[which, tile]] + product(slots[tile], unpack(masks[tile]))
        return 0

    lax.fori_loop(0, masks.shape[0] // UNROLL, group, 0)


def middle_phase(
    start, col, partial, features, grad_out, w_neigh, layer_out, grad_preact, upward_rows, weight_parts,
    own_part, scale, from_sibling, joined, arrived, own_sum, upward, mean_rows, parts, parts_arrived,
    keep_sem, sibling_send, sibling_recv, y_send, y_recv, up_send, up_recv, pass_send, pass_recv, w_send, w_recv,
):
    y, core = lax.div(col, 2), lax.rem(col, 2)
    ny, halves, rows = from_sibling.shape[:3]
    n_col = 2 * ny
    width = features.shape[1]
    place = [lax.rem(y + k, ny) for k in range(ny)]
    far_first = sorted(range(1, ny), key=lambda k: -min(k, ny - k))
    sibling = {"col": 2 * y + 1 - core}
    along_y = [{"col": 2 * place[k] + core} for k in range(ny)]
    along_col = [{"col": lax.rem(col + k, n_col)} for k in range(1, n_col)]
    pieces = [(half, k) for half in range(halves) for k in (*far_first, 0)]
    shared = {}
    for half, k in pieces:
        shared[half, k] = start(
            partial.at[4 * place[k] + 2 * (1 - core) + half], from_sibling.at[k, half],
            sibling_send, sibling_recv, half * ny + k, sibling,
        )
    exchanged = {}
    for half, k in pieces:
        shared[half, k].wait_recv()
        both = partial[4 * place[k] + 2 * core + half].astype(jnp.float32)
        both = both + from_sibling[k, half].astype(jnp.float32)
        if k == 0:
            own_sum[half] = both
        else:
            joined[k - 1, half] = both.astype(joined.dtype)
            exchanged[half, k] = start(
                joined.at[k - 1, half], arrived.at[k - 1, half],
                y_send, y_recv, half * (ny - 1) + k - 1, along_y[k],
            )
    gathered, passed, kept = {}, [], []
    for half in range(halves):
        summed = own_sum[half]
        for k in far_first:
            exchanged[half, k].wait_recv()
            summed = summed + arrived[k - 1, half].astype(jnp.float32)
        here = slice(half * rows, (half + 1) * rows)
        mean = (summed / scale[here]).astype(mean_rows.dtype)
        preact = own_part[here] + jnp.dot(mean, w_neigh[...], preferred_element_type=jnp.float32)
        sigmoid_values = jax.nn.sigmoid(preact)
        gradient = (
            grad_out[here].astype(jnp.float32) * sigmoid_values * (1.0 + preact * (1.0 - sigmoid_values))
        ).astype(grad_preact.dtype)
        sent_up = lax.dot_general(
            gradient, w_neigh[...], (((1,), (1,)), ((), ())), preferred_element_type=jnp.float32
        )
        upward[half] = (sent_up / scale[here]).astype(upward.dtype)
        target = upward_rows.at[2 * col + half]
        for k in far_first:
            gathered[half, k] = start(
                upward.at[half], target, up_send, up_recv, half * (ny - 1) + k - 1, along_y[k]
            )
        passed.append(start(upward.at[half], target, pass_send, pass_recv, half * ny, sibling))
        kept.append(pltpu.make_async_copy(upward.at[half], target, keep_sem.at[half]))
        kept[-1].start()
        layer_out[here] = (preact * sigmoid_values).astype(layer_out.dtype)
        mean_rows[here] = mean
        grad_preact[here] = gradient
    part_rows = width // n_col
    for which, source in enumerate((features, mean_rows)):
        product = lax.dot_general(
            source[...], grad_preact[...], (((0,), (0,)), ((), ())), preferred_element_type=jnp.float32
        ).astype(parts.dtype)
        for c in range(n_col):
            parts[c, which * part_rows : (which + 1) * part_rows] = product[
                c * part_rows : (c + 1) * part_rows
            ]
    reduced = [
        start(parts.at[lax.rem(col + k, n_col)], parts_arrived.at[k - 1], w_send, w_recv, k - 1, peer)
        for k, peer in enumerate(along_col, 1)
    ]
    for half in range(halves):
        for k in reversed(far_first):
            gathered[half, k].wait_recv()
            held = upward_rows.at[4 * lax.rem(y + ny - k, ny) + 2 * core + half]
            passed.append(start(held, held, pass_send, pass_recv, half * ny + k, sibling))
    total = parts[col].astype(jnp.float32)
    for k, each in enumerate(reduced):
        each.wait_recv()
        total = total + parts_arrived[k].astype(jnp.float32)
    weight_parts[...] = total.reshape(weight_parts.shape)
    for each in passed:
        each.wait_recv()
    for each in kept:
        each.wait()


def scatter_phase(
    start, torus, col, transfers, order, split, n_col, grad_scale, partial, round_owner, weight_parts, grad_preact, w_self,
    moved_in, weight_sums, arrived, self_grad, z_arrived, x_sums, z_sums,
    send_sem, recv_sem, z_send, z_recv, x_send, x_recv, zz_send, zz_recv, cc_send, cc_recv,
):
    nx, nz = torus.nx, torus.nz
    along_col = [{"col": lax.rem(col + k, n_col)} for k in range(1, n_col)]
    along_z = [{"row": torus.row(0, k)} for k in range(1, nz)]
    along_x = [{"row": torus.row(k, 0)} for k in range(1, nx)]

    def multiply_self(before):
        moved = jnp.dot(
            row_order(grad_preact.shape[0]), grad_preact[...], preferred_element_type=jnp.float32
        ).astype(jnp.bfloat16)
        self_grad[...] = lax.dot_general(
            moved, w_self[...], (((1,), (1,)), ((), ())), preferred_element_type=jnp.float32
        )
        return before

    def reduce_along_z(_):
        return [
            start(weight_parts.at[lax.rem(torus.z + k, nz)], z_arrived.at[k - 1], z_send, z_recv, k - 1, peer)
            for k, peer in enumerate(along_z, 1)
        ]

    def reduce_along_x(before):
        for each in before:
            each.wait_recv()
        part = weight_parts[torus.z]
        for k in range(nz - 1):
            part = part + z_arrived[k]
        x_sums[torus.x] = part
        return [
            start(x_sums.at[torus.x], x_sums.at[torus.x], x_send, x_recv, k, peer)
            for k, peer in enumerate(along_x)
        ]

    def gather_along_z(before):
        for each in before:
            each.wait_recv()
        part = x_sums[0]
        for k in range(1, nx):
            part = part + x_sums[k]
        z_sums[torus.z] = part * grad_scale
        return [
            start(z_sums.at[torus.z], z_sums.at[torus.z], zz_send, zz_recv, k, peer)
            for k, peer in enumerate(along_z)
        ]

    def gather_along_col(before):
        for each in before:
            each.wait_recv()
        weight_sums[col] = z_sums[...].reshape(weight_sums.shape[1:]).astype(weight_sums.dtype)
        return [
            start(weight_sums.at[col], weight_sums.at[col], cc_send, cc_recv, k, peer)
            for k, peer in enumerate(along_col)
        ]

    def carry(index, source):
        axis, sign, _, count, _ = transfers[index]
        return start(
            source,
            arrived.at[index, pl.ds(0, count)],
            send_sem,
            recv_sem,
            index,
            torus.neighbour(axis, -sign),
        )

    def sum_of(node, carried):
        _, first, full = split[node[0]]
        value = partial[torus.row(node[1], node[2]), first : first + full].astype(jnp.float32)
        for index in reversed(carried):
            lead, count = transfers[index][2:4]
            sent[index].wait_recv()
            came = arrived[index, :count].astype(jnp.float32)
            if count < full:
                filler = jnp.zeros((full - count, came.shape[1]), jnp.float32)
                came = jnp.concatenate([came, filler] if lead == first else [filler, came], axis=0)
            value = value + came
        return value

    sent = {}
    pending = []
    steps = [reduce_along_z, multiply_self, reduce_along_x, gather_along_z, gather_along_col]
    n_parts = len(split)
    inner = sum(1 for _, brought, carried in order if brought and carried)
    stages = {inner * at // 100: step for at, step in zip(STAGES, steps)}
    seen = 0
    rounded = set()
    for node, brought, carried in reversed(order[2 * n_parts :]):
        begin = split[node[0]][1]
        if node[1:] not in rounded:
            rounded.add(node[1:])
            round_owner(torus.row(*node[1:]))
        if carried:
            if seen in stages:
                pending = stages[seen](pending)
            seen += 1
            full = split[node[0]][2]
            home = next(index for index in carried if transfers[index][3] == full)
            if len(carried) == 1:
                sent[home].wait_recv()
                arrived[home, :full] += partial[torus.row(node[1], node[2]), begin : begin + full]
            else:
                arrived[home, :full] = sum_of(node, carried).astype(arrived.dtype)
        for index in reversed(brought):
            first, count = transfers[index][2:4]
            if carried:
                source = arrived.at[home, pl.ds(first - begin, count)]
            else:
                source = partial.at[torus.row(node[1], node[2]), pl.ds(first, count)]
            sent[index] = carry(index, source)

    round_owner(torus.row(0, 0))
    sums = []
    for (node, _, first_carried), (_, _, carried) in zip(order[:n_parts], order[n_parts:]):
        sums.append((split[node[0]][1], sum_of(node, first_carried + carried)))
    neighbour_sum = jnp.concatenate([part for _, part in sorted(sums, key=lambda pair: pair[0])], axis=0)
    moved_in[...] = (self_grad[...] + neighbour_sum).astype(moved_in.dtype)
    for each in pending:
        each.wait_recv()


def layer_kernel(
    transfers, order, split, nx, nz, n_col, grad_scale,
    slots, live, slots_in,
    features_in, grad_out_in, degrees_in, w_self_in, w_neigh_in, bias_in, masks_in,
    layer_out, moved_in, weight_sums,
    slots_row, features, grad_out, degrees, w_self, w_neigh, bias, masks,
    own, panel, sums, partial, grad_preact, upward_rows, weight_parts, spread,
    own_part, scale, from_sibling, joined, y_arrived, own_sum, upward, mean_rows, parts, parts_arrived,
    arrived, self_grad, z_arrived, x_sums, z_sums,
    chains, before, load_sem, own_sem, chain_sem, ring_send, ring_recv, back_send, back_recv, keep_sem, *sems,
):
    torus = Torus(nx, nz)
    col = lax.axis_index("col")
    start = Sender()
    loads = [
        pltpu.make_async_copy(source, target, load_sem.at[k])
        for k, (source, target) in enumerate(
            (
                (features_in, features),
                (slots_in, slots_row),
                (w_self_in, w_self),
                (degrees_in, degrees),
                (bias_in, bias),
                (grad_out_in, grad_out),
                (w_neigh_in, w_neigh),
                (masks_in, masks),
            )
        )
    ]
    for each in loads:
        each.start()
    barrier = pltpu.get_barrier_semaphore()
    around = [torus.neighbour(axis, sign) for axis in "xz" for sign in (1, -1)]
    around.append({"col": col + 1 - 2 * lax.rem(col, 2)})
    around += [{"col": lax.rem(col + k, n_col)} for k in range(2, n_col, 2)]
    greet(barrier, around)
    loads[0].wait()
    own[...] = jnp.dot(
        row_order(own.shape[0]), features[...], preferred_element_type=jnp.float32
    ).astype(own.dtype)
    keep = pltpu.make_async_copy(own, panel.at[torus.row(0, 0)], own_sem)
    keep.start()
    pl.semaphore_wait(barrier, len(around))

    roots = 2 * len(split)
    sent = gather_phase(start, torus, transfers, order[:roots], own, panel, ring_send, ring_recv, {})
    n_tiles, block_rows = masks.shape[0], partial.shape[0]
    loads[1].wait()
    write_chains(slots_row, live[0], block_rows, n_tiles, chains)
    tables = pltpu.make_async_copy(chains, before, chain_sem)
    tables.start()
    size, width = features.shape
    for each in loads[2:]:
        each.wait()
    scale[...] = jnp.broadcast_to(degrees[...].astype(jnp.float32), (width, size)).T
    own_part[...] = bias[...] + jnp.dot(
        features[...], w_self[...], preferred_element_type=jnp.float32
    )
    sums[0] = jnp.zeros(sums.shape[1:], sums.dtype)
    gather_phase(start, torus, transfers, order[roots:], own, panel, ring_send, ring_recv, sent)
    keep.wait()
    tables.wait()

    in_row = size // TILE

    def aggregate(slot, bits):
        block = lax.div(slot, block_rows)
        source = panel[lax.div(block, in_row), pl.ds(lax.rem(block, in_row) * TILE, TILE)]
        return lax.dot_general(bits, source, (((0,), (0,)), ((), ())), preferred_element_type=jnp.float32)

    chain_tiles(slots, before, 0, masks, sums, aggregate)
    for k in range(block_rows):
        partial[k] = sums[before[0, n_tiles + k]].astype(partial.dtype)

    middle_phase(
        start, col, partial, features, grad_out, w_neigh, layer_out, grad_preact, upward_rows, weight_parts,
        own_part, scale, from_sibling, joined, y_arrived, own_sum, upward, mean_rows, parts, parts_arrived,
        keep_sem, *sems[:10],
    )

    def spread_tile(slot, bits):
        return jnp.dot(bits, upward_rows[lax.rem(slot, block_rows)], preferred_element_type=jnp.float32)

    chain_tiles(slots, before, 1, masks, sums, spread_tile)

    def round_owner(owner):
        for k in range(in_row):
            last = before[1, n_tiles + owner * in_row + k]
            spread[owner, k * TILE : (k + 1) * TILE] = sums[last].astype(spread.dtype)

    scatter_phase(
        start, torus, col, transfers, order, split, n_col, grad_scale, spread, round_owner, weight_parts, grad_preact, w_self,
        moved_in, weight_sums, arrived, self_grad, z_arrived, x_sums, z_sums,
        back_send, back_recv, *sems[10:],
    )
    for each in start.started:
        each.wait_send()


def finish_kernel(layer_in, moved_in, weight_sums, layer_out, grad_in, grad_self, grad_neigh, layer_sem):
    hand_on = pltpu.make_async_copy(layer_in, layer_out, layer_sem)
    hand_on.start()
    grad_in[...] = lax.dot_general(
        row_order(moved_in.shape[0]), moved_in[...], (((0,), (0,)), ((), ())), preferred_element_type=jnp.float32
    ).astype(grad_in.dtype)
    rows = weight_sums.shape[1] // 2
    for c in range(weight_sums.shape[0]):
        grad_self[c * rows : (c + 1) * rows] = weight_sums[c, :rows].astype(grad_self.dtype)
        grad_neigh[c * rows : (c + 1) * rows] = weight_sums[c, rows:].astype(grad_neigh.dtype)
    hand_on.wait()


def array(dtype, *shape):
    return jax.ShapeDtypeStruct(shape, dtype)


def shards(features, grad_out, degrees, w_self, w_neigh, bias, tile_slots, tile_count, tile_masks):
    size, width = features.shape
    n_row, n_col = lax.axis_size("row"), lax.axis_size("col")
    nx, nz = 4, n_row // 4
    ny, halves = n_col // 2, size // TILE
    split = [("xz", 0, 48), ("xz", 48, 48), ("zx", 96, 80), ("zx", 176, 80)]
    transfers, order = torus_plan(nx, nz, split)
    copies = len(transfers)
    bf16, f32, i32 = jnp.bfloat16, jnp.float32, jnp.int32
    dma = pltpu.SemaphoreType.DMA
    slots, live, masks = tile_slots[0, 0], tile_count[0], tile_masks[0, 0]
    n_tiles = masks.shape[0]
    block_rows = n_col * halves
    block_columns = n_row * halves
    places = -(-(n_tiles + max(block_rows, block_columns)) // TILE) * TILE
    grad_scale = 1.0 / math.sqrt(size * n_row * n_col)
    grad_rows = 2 * width // n_col
    z_rows = grad_rows // nz
    others = n_col - 1
    y_copies = (ny - 1) * halves

    layer_in, moved_in, weight_sums = pl.pallas_call(
        functools.partial(layer_kernel, transfers, order, split, nx, nz, n_col, grad_scale),
        name="layer",
        out_shape=(
            array(bf16, size, width),
            array(bf16, size, width),
            array(bf16, n_col, grad_rows, width),
        ),
        in_specs=[SMEM, SMEM] + [ANY] * 8,
        out_specs=(VMEM, VMEM, VMEM),
        scratch_shapes=[
            pltpu.VMEM((1, n_tiles), i32),
            pltpu.VMEM((size, width), bf16),
            pltpu.VMEM((size, width), bf16),
            pltpu.VMEM((1, size), i32),
            pltpu.VMEM((width, width), bf16),
            pltpu.VMEM((width, width), bf16),
            pltpu.VMEM((1, width), f32),
            pltpu.VMEM(masks.shape, i32),
            pltpu.VMEM((size, width), bf16),
            pltpu.VMEM((n_row, size, width), bf16),
            pltpu.VMEM((n_tiles + 1, TILE, width), f32),
            pltpu.VMEM((block_rows, TILE, width), bf16),
            pltpu.VMEM((size, width), bf16),
            pltpu.VMEM((block_rows, TILE, width), bf16),
            pltpu.VMEM((nz, z_rows, width), f32),
            pltpu.VMEM((n_row, size, width), bf16),
            pltpu.VMEM((size, width), f32),
            pltpu.VMEM((size, width), f32),
            pltpu.VMEM((ny, halves, TILE, width), bf16),
            pltpu.VMEM((ny - 1, halves, TILE, width), bf16),
            pltpu.VMEM((ny - 1, halves, TILE, width), bf16),
            pltpu.VMEM((halves, TILE, width), f32),
            pltpu.VMEM((halves, TILE, width), bf16),
            pltpu.VMEM((size, width), bf16),
            pltpu.VMEM((n_col, grad_rows, width), bf16),
            pltpu.VMEM((others, grad_rows, width), bf16),
            pltpu.VMEM((copies, max(part[2] for part in split), width), bf16),
            pltpu.VMEM((size, width), f32),
            pltpu.VMEM((nz - 1, z_rows, width), f32),
            pltpu.VMEM((nx, z_rows, width), f32),
            pltpu.VMEM((nz, z_rows, width), f32),
            pltpu.VMEM((2, places), i32),
            pltpu.SMEM((2, places), i32),
            dma((8,)),
            dma,
            dma,
        ]
        + [dma((copies,))] * 4
        + [dma((halves,))]
        + [dma((ny * halves,))] * 2
        + [dma((y_copies,))] * 4
        + [dma((ny * halves,))] * 2
        + [dma((others,))] * 2
        + [dma((nz - 1,))] * 2
        + [dma((nx - 1,))] * 2
        + [dma((nz - 1,))] * 2
        + [dma((others,))] * 2,
        compiler_params=pltpu.CompilerParams(
            collective_id=0, has_side_effects=True, vmem_limit_bytes=58 << 20
        ),
    )(
        slots,
        live,
        slots[None, :],
        features,
        grad_out,
        degrees[None, :],
        w_self,
        w_neigh,
        bias[None, :],
        masks,
    )

    return pl.pallas_call(
        finish_kernel,
        name="finish",
        out_shape=(
            array(bf16, size, width),
            array(bf16, size, width),
            array(f32, width, width),
            array(f32, width, width),
        ),
        in_specs=[ANY, VMEM, VMEM],
        out_specs=(ANY, VMEM, VMEM, VMEM),
        scratch_shapes=[pltpu.SemaphoreType.DMA],
        compiler_params=pltpu.CompilerParams(vmem_limit_bytes=58 << 20),
    )(layer_in, moved_in, weight_sums)


def solution(mesh):
    placed = (
        P(("row", "col"), None),
        P(("row", "col"), None),
        P(("row", "col")),
        P(),
        P(),
        P(),
        P("row", "col", None),
        P("row", "col"),
        P("row", "col", None, None, None),
    )
    return jax.shard_map(
        shards,
        mesh=mesh,
        in_specs=placed,
        out_specs=(P(("row", "col"), None), P(("row", "col"), None), P(), P()),
        check_vma=False,
    )
```
